32 devices in a mesh: sec: 4 (over y, x), tile: 8 (over z, core).
Axes of the slice: x: 2, y: 2, z: 4, core: 2. Of those that a mesh axis runs over, the one named last changes fastest.
Arguments:
- atm_state: float32 [4, 32, 262144], P(None, None, ('sec', 'tile')), may hold values from -6 to 6
- diffusivity: float32 [32, 262144], P(None, ('sec', 'tile')), may hold values from 0.05 to 32
- surface_prev: float32 [4, 262144], P(None, ('sec', 'tile')), may hold values from -6 to 6
- flux_mix: float32 [10, 12], replicated, may hold values from -1.75 to 1.75
- entry_dest: int32 [2048, 1], P(('sec', 'tile')), may hold values from 0 to 31; in each aligned block of 64 rows (0 to 63, 64 to 127, ...) at most 4 rows name the same one
- entry_tile: int32 [2048], P(('sec', 'tile')), may hold values from 0 to 63
- entry_row: int32 [2048], P(('sec', 'tile')), may hold values from 0 to 63
- regrid_blocks: bfloat16 [2048, 128, 128], P(('sec', 'tile')), may hold values from -0.5 to 0.5
- ocean_state: float32 [4, 8, 256, 1024], P(None, None, 'sec', 'tile'), may hold values from -6 to 6
- land_mask: int32 [256, 1024], P('sec', 'tile'), may hold values 0 or 1
- flux_response: float32 [4, 10], replicated, may hold values from -2 to 2
Outputs:
- atm_next: float32 [4, 32, 262144], P(None, None, ('sec', 'tile'))
- ocean_next: float32 [4, 8, 256, 1024], P(None, None, 'sec', 'tile')
- surface_next: float32 [4, 262144], P(None, ('sec', 'tile'))
The draws below stay inside these ranges and needn't reach their ends.
Inputs may be any that keep to these rules, and one draw needn't show every extreme that they name: `entry_dest`: among the 64 entries of one device no destination is named more than 4 times, and in some device's entries one destination is named exactly 4 times; every device is named by some entry.
All inputs are finite; a program needn't handle non-finite values. No bound on the sum of `land_mask` on one device may be relied on, other than what follows from the above.
Results may differ from the reference program's by a relative error of at most 0.0003.
Values sent between devices are 32-bit elements; how exact they have to be, the bound alone decides.
No kernel may reach another device: no remote copies, remote signals or barrier semaphores. Data moves between devices by JAX's collectives and lax.ppermute only.
A program may use at most 128 MiB of HBM per device.

```python
import math
import jax
import jax.numpy as jnp
import numpy as np
from jax import lax

LEV = 32
OLEV = 8
TA = 128
TO = 128
CAP = 4
ATILES = 64
OX = 64
NCOL = 262144
ENTRIES = 64
NENT = 2048
NX = 256
NY = 1024
N_SEC = 4
N_TILE = 8


def draw_atm_state(key, part):
    key_rough = jax.random.fold_in(key, 11)
    key_slope = jax.random.fold_in(key, 12)
    level = lax.broadcasted_iota(jnp.float32, (1, LEV, 1), 1)
    height = 2.0 * level / float(max(LEV - 1, 1)) - 1.0
    rough = jnp.clip(jax.random.normal(key_rough, (4, LEV, NCOL), jnp.float32), -3.0, 3.0)
    slope = jax.random.uniform(key_slope, (4, 1, NCOL), jnp.float32, -1.0, 1.0)
    return (rough + 3.0 * slope * height).astype(jnp.float32)


def draw_diffusivity(key, part):
    key_surface = jax.random.fold_in(key, 21)
    key_upper = jax.random.fold_in(key, 22)
    fraction = jax.random.uniform(key_surface, (1, NCOL), jnp.float32, 0.0, 1.0)
    surface_rate = jnp.exp(math.log(0.05) + fraction * math.log(80.0))
    upper_frac = jax.random.uniform(key_upper, (LEV - 1, NCOL), jnp.float32, 0.0, 1.0)
    upper_rate = jnp.exp(math.log(8.0) + upper_frac * math.log(4.0))
    return jnp.concatenate([surface_rate, upper_rate], 0).astype(jnp.float32)


def place_ends(result, stream_key, smallest, high):
    longest = result.shape.index(max(result.shape))
    spots = []
    for shift in (0, 1):
        where = [jax.random.randint(jax.random.fold_in(stream_key, axis), (), 0, length) for axis, length in enumerate(result.shape)]
        where[longest] = (where[longest] + shift) % result.shape[longest]
        spots.append(tuple(where))
    return result.at[spots[0]].set(smallest).at[spots[1]].set(high)


def steps_of(stream_key, dims, cuts, least, top_value):
    gain, own = 1.0, jax.random.fold_in(stream_key, 6)
    for dim, blocks in cuts:
        steps = jnp.exp(jax.random.uniform(jax.random.fold_in(own, dim), (blocks,), jnp.float32, least / len(cuts), top_value / len(cuts)))
        gain = gain * jnp.repeat(steps, dims[dim] // blocks).reshape([-1 if axis == dim else 1 for axis in range(len(dims))])
    return gain


def shared_out(stream_key, own, number, rows, number_of, top, most, skew):
    sequence = jax.random.permutation(stream_key, number_of)
    heavy_load, ordinary = portions_of(number_of, rows * top, most, skew, True), portions_of(number_of, rows * top, most, skew, False)
    places = jnp.arange(number_of)

    def named(lengths, offset_by):
        used = int((lengths > 0).sum())
        fixed = max(1, used // 4)
        shifted = fixed + (places - fixed + offset_by * (used - fixed)) % max(1, number_of - fixed)
        return jnp.zeros((number_of,), jnp.int32).at[sequence[jnp.where(places < fixed, places, shifted)]].set(jnp.asarray(lengths, jnp.int32))

    lengths = jnp.where(number % 4 == 0, named(heavy_load, number // 4), named(ordinary, number - number // 4 - 1))
    mixed = jax.random.permutation(jax.random.fold_in(own, 3), number_of)
    donor, receiver = mixed[0:number_of // 2 * 2:2], mixed[1:number_of // 2 * 2:2]
    margin = jnp.minimum(lengths[donor] - 1, most - lengths[receiver]) // 2
    margin = jnp.where((donor == sequence[0]) | (receiver == sequence[0]) | (lengths[receiver] == 0), 0, jnp.maximum(margin, 0))
    shifted = jax.random.randint(jax.random.fold_in(own, 4), (number_of // 2,), 0, 1 << 20) % (margin + 1)
    lengths = lengths.at[donor].add(-shifted).at[receiver].add(shifted)
    labels = jnp.searchsorted(jnp.cumsum(lengths), jnp.arange(rows * top), side="right").astype(jnp.int32)
    table = labels.reshape(top, rows).T
    table = table[jax.random.permutation(jax.random.fold_in(own, 1), rows)]
    offset_by = jax.random.randint(jax.random.fold_in(own, 2), (rows, 1), 0, top)
    return jnp.take_along_axis(table, (jnp.arange(top)[None, :] + offset_by) % top, axis=1)


def portions_of(count, total, bound, lean, full):
    loads = [(1 << 20) // math.isqrt(grade ** lean) + 1 for grade in range(1, count + 1)]
    largest = bound if full else min(bound, max(-(-total // count), total * loads[0] // sum(loads)))
    least = 1 if total - largest >= count - 1 else 0
    given, surplus = [largest] + [least] * (count - 1), total - largest - least * (count - 1)
    while surplus > 0:
        free = [i for i in range(1, count) if given[i] < largest] or [i for i in range(1, count) if given[i] < bound]
        whole, budget = sum([loads[i] for i in free]), surplus
        for i in free:
            more = min(bound - given[i], max(1, budget * loads[i] // whole), surplus)
            given[i] = given[i] + more
            surplus = surplus - more
    return np.array(given)


def scatter_about(own_key, dims, width, reach, cuts=(), dtype=jnp.bfloat16):
    factor_of = steps_of(own_key, dims, cuts, -0.22, 0.18) if cuts else 1.0
    entries = jax.random.normal(own_key, dims, jnp.float32) * width * factor_of
    return jnp.minimum(jnp.maximum(entries, -reach), reach).astype(dtype)


def setup_inputs(seed: int = 0) -> dict:
    splits = jax.random.split(jax.random.key(seed), 12)
    atm_state = draw_atm_state(jax.random.fold_in(splits[11], 71), 0)
    diffusivity = draw_diffusivity(jax.random.fold_in(splits[11], 71), 0)
    surface_prev = scatter_about(splits[2], (4, NCOL), 1.0, 6.0, ((1, 32),), jnp.float32)
    flux_mix = scatter_about(splits[3], (10, 12), 12 ** -0.5, 1.75, (), jnp.float32)
    entry_dest_keys = jax.random.split(jax.random.fold_in(splits[4], 1), NENT // ENTRIES)
    entry_dest_turns = jax.random.permutation(jax.random.fold_in(splits[4], 3), NENT // ENTRIES)
    entry_dest = jax.vmap(lambda own, number: shared_out(jax.random.fold_in(splits[4], 2), own, number, ENTRIES, N_SEC * N_TILE, 1, CAP, 2))(entry_dest_keys, entry_dest_turns).reshape((NENT, 1))
    entry_tile = place_ends(jax.random.randint(splits[5], (NENT,), 0, ATILES), jax.random.fold_in(splits[5], 1), 0, ATILES - 1).astype(jnp.int32)
    entry_row = place_ends(jax.random.randint(splits[6], (NENT,), 0, OX), jax.random.fold_in(splits[6], 1), 0, OX - 1).astype(jnp.int32)
    regrid_blocks = scatter_about(splits[7], (NENT, TA, TO), TA ** -0.5, 0.5, ((0, 32),))
    ocean_state = scatter_about(splits[8], (4, OLEV, NX, NY), 1.0, 6.0, ((2, 4), (3, 8)), jnp.float32)
    land_mask = place_ends((jax.random.randint(splits[9], (NX, NY), 0, 4) < 3).astype(jnp.int32), jax.random.fold_in(splits[9], 1), 0, 1)
    flux_response = scatter_about(splits[10], (4, 10), 10 ** -0.5, 2.0, (), jnp.float32)
    return {"atm_state": atm_state, "diffusivity": diffusivity, "surface_prev": surface_prev, "flux_mix": flux_mix, "entry_dest": entry_dest, "entry_tile": entry_tile, "entry_row": entry_row, "regrid_blocks": regrid_blocks, "ocean_state": ocean_state, "land_mask": land_mask, "flux_response": flux_response}


PRECISE = lax.Precision.HIGHEST
DIFFUSE = 0.2
CORIOLIS = 0.3
OCEAN_DT = 0.2


def boundary_layer(atmos_state, coupling, surface_value):
    levels = atmos_state.shape[1]
    coupling_up = jnp.concatenate([coupling[1:], jnp.zeros_like(coupling[:1])], 0)
    diagonal = 1.0 + coupling + coupling_up
    c_list = []
    d_list = []
    c_prev = -coupling_up[0] / diagonal[0]
    d_prev = (atmos_state[:, 0] + coupling[0] * surface_value) / diagonal[0]
    c_list.append(c_prev)
    d_list.append(d_prev)
    for lev_index in range(1, levels):
        coupling_low = -coupling[lev_index]
        pivot_value = diagonal[lev_index] - coupling_low * c_prev
        c_prev = -coupling_up[lev_index] / pivot_value
        d_prev = (atmos_state[:, lev_index] - coupling_low * d_prev) / pivot_value
        c_list.append(c_prev)
        d_list.append(d_prev)
    solved = d_list[levels - 1]
    solved_levels = [solved]
    for lev_index in range(levels - 2, -1, -1):
        solved = d_list[lev_index] - c_list[lev_index] * solved
        solved_levels.append(solved)
    updated_state = jnp.stack(solved_levels[::-1], axis=1)
    turbulent = coupling[0] * (surface_value - updated_state[:, 0])
    features = jnp.concatenate([turbulent, updated_state[:, 0], turbulent * updated_state[:, 1]], 0)
    return updated_state, features


def ocean_update(padded, forcing, ocean_depth):
    mask_grid = padded[-1]
    fields = padded[:-1].reshape(4, ocean_depth, padded.shape[1], padded.shape[2])
    centre = fields[:, :, 1:-1, 1:-1]
    east_cells = fields[:, :, 2:, 1:-1]
    west_cells = fields[:, :, :-2, 1:-1]
    north_cells = fields[:, :, 1:-1, 2:]
    south_cells = fields[:, :, 1:-1, :-2]
    laplace = mask_grid[2:, 1:-1] * (east_cells - centre) + mask_grid[:-2, 1:-1] * (west_cells - centre)
    laplace = laplace + mask_grid[1:-1, 2:] * (north_cells - centre) + mask_grid[1:-1, :-2] * (south_cells - centre)
    zonal_flow = centre[2]
    merid_flow = centre[3]
    advect = 0.5 * (zonal_flow * (east_cells - west_cells) + merid_flow * (north_cells - south_cells))
    nothing = jnp.zeros_like(zonal_flow)
    rotation = jnp.stack([nothing, nothing, CORIOLIS * merid_flow, -CORIOLIS * zonal_flow])
    tendency = DIFFUSE * laplace - advect + rotation
    surface_on = (lax.broadcasted_iota(jnp.int32, (1, ocean_depth, 1, 1), 1) == 0).astype(jnp.float32)
    updated = centre + OCEAN_DT * tendency + forcing[:, None] * surface_on
    return mask_grid[1:-1, 1:-1] * updated


def reference(atm_state, diffusivity, surface_prev, flux_mix, entry_dest, entry_tile, entry_row, regrid_blocks, ocean_state, land_mask, flux_response):
    devices = N_SEC * N_TILE
    atm_next, features = boundary_layer(atm_state, diffusivity, surface_prev)
    fluxes = jnp.dot(flux_mix, features, precision=PRECISE)
    flux_dev = fluxes.reshape(10, devices, ATILES, TA).transpose(1, 2, 0, 3)
    dest_all = entry_dest[:, 0].reshape(devices, ENTRIES)
    tile_all = entry_tile.reshape(devices, ENTRIES)
    row_all = entry_row.reshape(devices, ENTRIES)
    block_all = regrid_blocks.reshape(devices, ENTRIES, TA, TO)

    def forward(gathered, inputs):
        flux_tiles, dest_ids, tile_ids, row_ids, blocks = inputs
        picked = flux_tiles[tile_ids]
        contrib = jnp.einsum('efa,eat->eft', picked, blocks.astype(jnp.float32), precision=PRECISE)
        return gathered.at[dest_ids, row_ids].add(contrib), None

    empty_flux = jnp.zeros((devices, OX, 10, TO), jnp.float32)
    ocean_flux, unused = lax.scan(forward, empty_flux, (flux_dev, dest_all, tile_all, row_all, block_all))
    grid_flux = ocean_flux.reshape(N_SEC, N_TILE, OX, 10, TO).transpose(3, 0, 2, 1, 4).reshape(10, NX, NY)
    bulk_arg = jnp.einsum('kf,kxy->fxy', flux_response, ocean_state[:, 0], precision=PRECISE)
    bulk = 1.0 + 0.5 * jnp.tanh(bulk_arg)
    forcing = jnp.einsum('gf,fxy->gxy', flux_response, grid_flux * bulk, precision=PRECISE)
    stacked = jnp.concatenate([ocean_state.reshape(4 * OLEV, NX, NY), land_mask.astype(jnp.float32)[None]], 0)
    padded = jnp.pad(stacked, ((0, 0), (1, 1), (1, 1)))
    ocean_next = ocean_update(padded, forcing, OLEV)
    surface_dev = ocean_next[:, 0].reshape(4, N_SEC, OX, N_TILE, TO).transpose(1, 3, 2, 0, 4).reshape(devices, OX, 4, TO)

    def backward(inputs):
        dest_ids, tile_ids, row_ids, blocks = inputs
        rows_got = surface_dev[dest_ids, row_ids]
        regridded = jnp.einsum('eft,eat->efa', rows_got, blocks.astype(jnp.float32), precision=PRECISE)
        return jnp.zeros((ATILES, 4, TA), jnp.float32).at[tile_ids].add(regridded)

    surf_dev = lax.map(backward, (dest_all, tile_all, row_all, block_all))
    surface_next = surf_dev.transpose(2, 0, 1, 3).reshape(4, NCOL)
    return atm_next, ocean_next, surface_next
```

```python
import functools

import jax
import jax.numpy as jnp
from jax import lax
from jax.experimental import pallas as pl
from jax.experimental.pallas import tpu as pltpu
from jax.sharding import PartitionSpec as P

CAP = 4
LANES = 128
SUB = 8
FLUXES = 10
FEATURES = 12
FIELDS = 4
DIFFUSE = 0.2
CORIOLIS = 0.3
OCEAN_DT = 0.2
F32 = jnp.float32
BF16 = jnp.bfloat16
BOTH = ("sec", "tile")


def halves(x):
    high = x.astype(BF16)
    return high, (x - high.astype(F32)).astype(BF16)


def dot32(a, b):
    return jnp.dot(a, b, preferred_element_type=F32)


def spec_any():
    return pl.BlockSpec(memory_space=pltpu.HBM)


def spec_vmem():
    return pl.BlockSpec(memory_space=pltpu.VMEM)


def spec_smem():
    return pl.BlockSpec(memory_space=pltpu.SMEM)


def params(mib):
    return pltpu.CompilerParams(vmem_limit_bytes=mib * 2**20)


def atm_kernel(
    chunks,
    a_ref,
    d_ref,
    s_ref,
    mix_ref,
    dest_ref,
    tile_ref,
    w_ref,
    y_ref,
    e_ref,
    out_ref,
    a_buf,
    d_buf,
    s_buf,
    w_buf,
    y_buf,
    e_buf,
    flux,
    count,
    in_sems,
    out_sems,
    s_sem,
    w_sem,
):
    blocks, tiles = a_buf.shape[1], a_buf.shape[2]
    levels = blocks * SUB
    entries = w_buf.shape[0]
    per = tiles // chunks
    groups = per // SUB
    devices = count.shape[0]

    def loads(ci):
        at = pl.ds(ci * per, per)
        return (
            pltpu.make_async_copy(a_ref.at[:, :, at], a_buf.at[:, :, at], in_sems.at[ci, 0]),
            pltpu.make_async_copy(d_ref.at[:, at], d_buf.at[:, at], in_sems.at[ci, 1]),
        )

    def saves(ci):
        at = pl.ds(ci * per, per)
        return (
            pltpu.make_async_copy(y_buf.at[:, :, at], y_ref.at[:, :, at], out_sems.at[ci, 0]),
            pltpu.make_async_copy(e_buf.at[:, at], e_ref.at[:, at], out_sems.at[ci, 1]),
        )

    s_copy = pltpu.make_async_copy(s_ref, s_buf, s_sem)
    w_copy = pltpu.make_async_copy(w_ref, w_buf, w_sem)
    for copy in loads(0):
        copy.start()
    s_copy.start()
    for ci in range(1, chunks):
        for copy in loads(ci):
            copy.start()
    w_copy.start()

    a_rows = a_buf.reshape(FIELDS * blocks * tiles * SUB, LANES)
    d_rows = d_buf.reshape(blocks * tiles * SUB, LANES)
    s_copy.wait()
    for d in range(devices):
        count[d] = 0
    out_ref[...] = jnp.zeros_like(out_ref)

    def chunk(ci, _):
        for copy in loads(ci):
            copy.wait()
        first = ci * per

        def block(step, carry):
            lb = blocks - 1 - step
            bottom = jnp.where(lb == 0, 1.0, 0.0).astype(F32)
            carry = list(carry)
            for r in range(SUB - 1, -1, -1):
                for g in range(groups):
                    tile = first + g * SUB
                    grow, above, ys = carry[g]
                    coup = d_rows[pl.ds((lb * tiles + tile) * SUB + r, SUB, stride=SUB), :]
                    weight = 1.0 + above * grow
                    inverse = 1.0 / (weight + coup)
                    solved = []
                    for v in range(FIELDS):
                        row = ((v * blocks + lb) * tiles + tile) * SUB + r
                        rhs = a_rows[pl.ds(row, SUB, stride=SUB), :]
                        if r == 0:
                            rhs = rhs + coup * (s_buf[v, pl.ds(tile, SUB), :] * bottom)
                        value = (rhs + above * ys[v]) * inverse
                        y_buf[v, lb * SUB + r, pl.ds(tile, SUB), :] = value
                        solved.append(value)
                    e_buf[lb * SUB + r, pl.ds(tile, SUB), :] = coup * inverse
                    carry[g] = (weight * inverse, coup, tuple(solved))
            return tuple(carry)

        zero = jnp.zeros((SUB, LANES), F32)
        start = tuple((zero, zero, (zero,) * FIELDS) for _ in range(groups))
        final = lax.fori_loop(0, blocks, block, start)
        for copy in saves(ci):
            copy.start()
        for g in range(groups):
            tile = first + g * SUB
            _, coup, x0 = final[g]
            e1 = e_buf[1, pl.ds(tile, SUB), :]
            turb = [coup * (s_buf[v, pl.ds(tile, SUB), :] - x0[v]) for v in range(FIELDS)]
            x1 = [y_buf[v, 1, pl.ds(tile, SUB), :] + e1 * x0[v] for v in range(FIELDS)]
            feats = turb + list(x0) + [turb[v] * x1[v] for v in range(FIELDS)]
            for f in range(FLUXES):
                total = mix_ref[f, 0] * feats[0]
                for k in range(1, FEATURES):
                    total = total + mix_ref[f, k] * feats[k]
                flux[pl.ds(tile * 16 + f, SUB, stride=16), :] = total
        return 0

    lax.fori_loop(0, chunks, chunk, 0)
    w_copy.wait()

    def entry(e, _):
        d = dest_ref[e, 0]
        k = count[d]
        count[d] = k + 1
        picked = flux[pl.ds(pl.multiple_of(tile_ref[e] * 16, 16), 16), :]
        high, low = halves(picked)
        both = dot32(jnp.concatenate([high, low], axis=0), w_buf[e])
        both = both[:16] + both[16:]
        row = d * (FLUXES * CAP) + k
        out_ref[pl.ds(row, SUB, stride=CAP), :] = both[:SUB]
        out_ref[pl.ds(row + SUB * CAP, FLUXES - SUB, stride=CAP), :] = both[SUB:FLUXES]
        return 0

    lax.fori_loop(0, entries, entry, 0, unroll=8)
    for ci in range(chunks):
        for copy in saves(ci):
            copy.wait()


def atm_forward(a_tiles, d_tiles, s_tiles, mix, dest, tile_ids, weights, devices):
    _, blocks, tiles, _, _ = a_tiles.shape
    levels = blocks * SUB
    entries = weights.shape[0]
    chunks = 2
    return pl.pallas_call(
        functools.partial(atm_kernel, chunks),
        out_shape=(
            jax.ShapeDtypeStruct((FIELDS, levels, tiles, LANES), F32),
            jax.ShapeDtypeStruct((levels, tiles, LANES), F32),
            jax.ShapeDtypeStruct((devices * FLUXES * CAP, LANES), F32),
        ),
        in_specs=[
            spec_any(),
            spec_any(),
            spec_any(),
            spec_smem(),
            spec_smem(),
            spec_smem(),
            spec_any(),
        ],
        out_specs=(spec_any(), spec_any(), spec_vmem()),
        scratch_shapes=[
            pltpu.VMEM(a_tiles.shape, F32),
            pltpu.VMEM(d_tiles.shape, F32),
            pltpu.VMEM(s_tiles.shape, F32),
            pltpu.VMEM(weights.shape, BF16),
            pltpu.VMEM((FIELDS, levels, tiles, LANES), F32),
            pltpu.VMEM((levels, tiles, LANES), F32),
            pltpu.VMEM((tiles * 16, LANES), F32),
            pltpu.SMEM((devices,), jnp.int32),
            pltpu.SemaphoreType.DMA((chunks, 2)),
            pltpu.SemaphoreType.DMA((chunks, 2)),
            pltpu.SemaphoreType.DMA,
            pltpu.SemaphoreType.DMA,
        ],
        compiler_params=params(48),
        name="atm_forward",
    )(a_tiles, d_tiles, s_tiles, mix, dest, tile_ids, weights)


def back_kernel(y_ref, e_ref, out_ref):
    blocks, tiles = out_ref.shape[1], out_ref.shape[2]
    rows = out_ref.reshape(FIELDS * blocks * tiles * SUB, LANES)
    groups = tiles // SUB

    def block(lb, carry):
        carry = list(carry)
        for r in range(SUB):
            for g in range(groups):
                coef = e_ref[lb * SUB + r, pl.ds(g * SUB, SUB), :]
                if r == 0:
                    coef = coef * jnp.where(lb == 0, 0.0, 1.0).astype(F32)
                for v in range(FIELDS):
                    x = y_ref[v, lb * SUB + r, pl.ds(g * SUB, SUB), :]
                    x = x + coef * carry[g * FIELDS + v]
                    row = ((v * blocks + lb) * tiles + g * SUB) * SUB + r
                    rows[pl.ds(row, SUB, stride=SUB), :] = x
                    carry[g * FIELDS + v] = x
        return tuple(carry)

    zero = jnp.zeros((SUB, LANES), F32)
    lax.fori_loop(0, blocks, block, (zero,) * (groups * FIELDS))


def atm_back(y, e):
    _, levels, tiles, _ = y.shape
    blocks = levels // SUB
    per = 16
    return pl.pallas_call(
        back_kernel,
        grid=(tiles // per,),
        out_shape=jax.ShapeDtypeStruct((FIELDS, blocks, tiles, SUB, LANES), F32),
        in_specs=[
            pl.BlockSpec((FIELDS, levels, per, LANES), lambda i: (0, 0, i, 0)),
            pl.BlockSpec((levels, per, LANES), lambda i: (0, i, 0)),
        ],
        out_specs=pl.BlockSpec((FIELDS, blocks, per, SUB, LANES), lambda i: (0, 0, i, 0, 0)),
        compiler_params=params(32),
        cost_estimate=pl.CostEstimate(
            flops=2 * y.size, bytes_accessed=9 * y.size, transcendentals=0
        ),
        name="atm_back",
    )(y, e)


def edge_kernel(
    q_ref, m_ref, dest_ref, row_ref, low_row, high_row, low_col, high_col, table, slots, count
):
    sec, tile = lax.axis_index("sec"), lax.axis_index("tile")
    me = sec * lax.axis_size("tile") + tile
    fields, rows, _ = q_ref.shape
    devices = count.shape[0]
    entries = row_ref.shape[0]
    pad = low_row.shape[0]
    lane_rows = table.shape[1]
    mask = m_ref[...].astype(F32)

    for dst, at in ((low_row, 0), (high_row, rows - 1)):
        dst[...] = jnp.zeros_like(dst)
        for i in range(fields):
            dst[i : i + 1, :] = q_ref[i, at : at + 1, :]
        dst[fields : fields + 1, :] = mask[at : at + 1, :]

    lane = lax.broadcasted_iota(jnp.int32, (SUB, LANES), 1)
    sub = lax.broadcasted_iota(jnp.int32, (SUB, LANES), 0)
    pick = ((sub == 0) & (lane == 0)) | ((sub == 1) & (lane == LANES - 1))
    pick = pick.astype(F32)
    low_col[...] = jnp.zeros_like(low_col)
    high_col[...] = jnp.zeros_like(high_col)
    for i in range(fields + 1):
        cells = q_ref[i] if i < fields else mask
        ends = lax.dot_general(
            pick,
            cells,
            (((1,), (1,)), ((), ())),
            precision=lax.Precision.HIGHEST,
            preferred_element_type=F32,
        )
        low_col[i : i + 1, 0:rows] = ends[0:1]
        high_col[i : i + 1, 0:rows] = ends[1:2]

    table[...] = jnp.zeros_like(table)
    for d in range(devices):
        count[d] = 0
    spot = lax.broadcasted_iota(jnp.int32, (lane_rows, LANES), 0) * LANES
    spot = spot + lax.broadcasted_iota(jnp.int32, (lane_rows, LANES), 1)

    def entry(e, _):
        d = dest_ref[e, 0]
        k = count[d]
        count[d] = k + 1
        slots[e] = d * CAP + k
        here = me * (2 * CAP) + k
        hit = (spot == here) | (spot == here + CAP)
        table[d] = table[d] + jnp.where(hit, row_ref[e] + 1, 0)
        return 0

    lax.fori_loop(0, entries, entry, 0)


def ocean_edges(q, mask, dest, row_ids, devices):
    pad = -(-(q.shape[0] + 1) // SUB) * SUB
    edge = jax.ShapeDtypeStruct((pad, LANES), F32)
    lane_rows = devices * 2 * CAP // LANES
    return pl.pallas_call(
        edge_kernel,
        out_shape=(edge,) * 4
        + (
            jax.ShapeDtypeStruct((devices, lane_rows, LANES), jnp.int32),
            jax.ShapeDtypeStruct((row_ids.shape[0],), jnp.int32),
        ),
        in_specs=[spec_vmem(), spec_vmem(), spec_smem(), spec_smem()],
        out_specs=(spec_vmem(),) * 5 + (spec_smem(),),
        scratch_shapes=[pltpu.SMEM((devices,), jnp.int32)],
        compiler_params=params(32),
        name="ocean_edges",
    )(q, mask, dest, row_ids)


def shift(axis, step):
    count = lax.axis_size(axis)
    if step > 0:
        return [(i, i + 1) for i in range(count - 1)]
    return [(i + 1, i) for i in range(count - 1)]


def ocean_kernel(
    depth,
    q_ref,
    m_ref,
    east_ref,
    west_ref,
    north_ref,
    south_ref,
    table_ref,
    resp_ref,
    out_ref,
    surf_ref,
    bulk_ref,
    hot_ref,
    hot_t_ref,
    col_buf,
):
    fields, rows, _ = q_ref.shape
    pad = north_ref.shape[0]
    lane_rows = table_ref.shape[1]
    col_buf[...] = jnp.zeros_like(col_buf)
    col_buf[0, 0:pad, :] = north_ref[...]
    col_buf[1, 0:pad, :] = south_ref[...]
    north_t = jnp.transpose(col_buf[0])[0:rows]
    south_t = jnp.transpose(col_buf[1])[0:rows]
    lane = lax.broadcasted_iota(jnp.int32, (rows, LANES), 1)
    last, first = lane == LANES - 1, lane == 0

    def around(cells, i):
        east = jnp.concatenate([cells[1:], east_ref[i : i + 1, :]], axis=0)
        west = jnp.concatenate([west_ref[i : i + 1, :], cells[:-1]], axis=0)
        north = jnp.where(last, north_t[:, i : i + 1], pltpu.roll(cells, LANES - 1, 1))
        south = jnp.where(first, south_t[:, i : i + 1], pltpu.roll(cells, 1, 1))
        return east, west, north, south

    mask = m_ref[...].astype(F32)
    m_east, m_west, m_north, m_south = around(mask, fields)
    m_all = m_east + m_west + m_north + m_south
    for level in range(depth):
        zonal = q_ref[2 * depth + level]
        merid = q_ref[3 * depth + level]
        for v in range(FIELDS):
            i = v * depth + level
            cells = q_ref[i]
            east, west, north, south = around(cells, i)
            lap = m_east * east + m_west * west + m_north * north + m_south * south
            lap = lap - m_all * cells
            adv = 0.5 * (zonal * (east - west) + merid * (north - south))
            tend = DIFFUSE * lap - adv
            if v == 2:
                tend = tend + CORIOLIS * merid
            if v == 3:
                tend = tend - CORIOLIS * zonal
            value = mask * (cells + OCEAN_DT * tend)
            out_ref[i] = value
            if level == 0:
                surf_ref[v] = value

    tops = [q_ref[v * depth] for v in range(FIELDS)]
    for f in range(FLUXES):
        total = resp_ref[0, f] * tops[0]
        for v in range(1, FIELDS):
            total = total + resp_ref[v, f] * tops[v]
        bulk_ref[f] = 1.0 + 0.5 * jnp.tanh(total)

    seen = jnp.sum(table_ref[...], axis=0)
    x = lax.broadcasted_iota(jnp.int32, (2 * rows, LANES), 0)
    spot = lax.broadcasted_iota(jnp.int32, (2 * rows, LANES), 1)
    pair = (spot // CAP) % 2 == x // rows
    for j in range(lane_rows):
        hot = (seen[j : j + 1, :] - 1 == x % rows) & pair
        hot = hot.astype(F32)
        hot_ref[:, j * LANES : (j + 1) * LANES] = hot.astype(BF16)
        hot_t_ref[j * LANES : (j + 1) * LANES, :] = jnp.transpose(hot).astype(BF16)


def ocean_step(q, mask, edges, table, response, depth):
    fields, rows, _ = q.shape
    slots = table.shape[0] * 2 * CAP
    return pl.pallas_call(
        functools.partial(ocean_kernel, depth),
        out_shape=(
            jax.ShapeDtypeStruct(q.shape, F32),
            jax.ShapeDtypeStruct((FIELDS, rows, LANES), F32),
            jax.ShapeDtypeStruct((FLUXES, rows, LANES), F32),
            jax.ShapeDtypeStruct((2 * rows, slots), BF16),
            jax.ShapeDtypeStruct((slots, 2 * rows), BF16),
        ),
        in_specs=[spec_vmem()] * 7 + [spec_smem()],
        out_specs=(spec_vmem(),) * 5,
        scratch_shapes=[pltpu.VMEM((2, LANES, LANES), F32)],
        compiler_params=params(32),
        name="ocean_step",
    )(q, mask, *edges, table, response)


def combine_kernel(
    depth, got_ref, hot_ref, hot_t_ref, bulk_ref, surf_ref, m_ref, resp_ref, q_ref,
    out_ref, back_ref, top, sems,
):
    rows = m_ref.shape[0]
    sources = got_ref.shape[0]
    force = [None] * FIELDS
    hot = hot_ref[...]
    for j in range(FLUXES // 2):
        data = got_ref[:, j * SUB : (j + 1) * SUB, :].reshape(sources * SUB, LANES)
        high, low = halves(data)
        both = dot32(hot, high) + dot32(hot, low)
        for p in range(2):
            f = 2 * j + p
            drive = both[p * rows : (p + 1) * rows] * bulk_ref[f]
            for g in range(FIELDS):
                term = resp_ref[g, f] * drive
                force[g] = term if f == 0 else force[g] + term
    mask = m_ref[...].astype(F32)
    for g in range(FIELDS):
        top[g] = surf_ref[g] + mask * force[g]
    copies = [
        pltpu.make_async_copy(top.at[g], out_ref.at[g * depth], sems.at[g]) for g in range(FIELDS)
    ]
    for copy in copies:
        copy.start()
    hot_t = hot_t_ref[...]
    for j in range(FIELDS // 2):
        pair = jnp.concatenate([top[2 * j], top[2 * j + 1]], axis=0)
        high, low = halves(pair)
        both = dot32(hot_t, high) + dot32(hot_t, low)
        back_ref[:, j * SUB : (j + 1) * SUB, :] = both.reshape(sources, SUB, LANES)
    for copy in copies:
        copy.wait()


def ocean_combine(got, hot, hot_t, bulk, surf, mask, response, q_next, depth):
    sources = got.shape[0]
    return pl.pallas_call(
        functools.partial(combine_kernel, depth),
        out_shape=(
            jax.ShapeDtypeStruct(q_next.shape, F32),
            jax.ShapeDtypeStruct((sources, FIELDS * CAP, LANES), F32),
        ),
        in_specs=[spec_vmem()] * 6 + [spec_smem(), spec_any()],
        out_specs=(spec_any(), spec_vmem()),
        scratch_shapes=[
            pltpu.VMEM(surf.shape, F32),
            pltpu.SemaphoreType.DMA((FIELDS,)),
        ],
        input_output_aliases={7: 0},
        compiler_params=params(32),
        name="ocean_combine",
    )(got, hot, hot_t, bulk, surf, mask, response, q_next)


def regrid_kernel(got_ref, w_ref, slot_ref, tile_ref, out_ref):
    entries = w_ref.shape[0]
    out_ref[...] = jnp.zeros_like(out_ref)

    def group(i, _):
        results = []
        for u in range(SUB):
            e = i * SUB + u
            slot = slot_ref[e]
            row = (slot // CAP) * (FIELDS * CAP) + slot % CAP
            rows = got_ref[pl.ds(row, FIELDS, stride=CAP), :]
            high, low = halves(rows)
            both = lax.dot_general(
                jnp.concatenate([high, low], axis=0),
                w_ref[e],
                (((1,), (1,)), ((), ())),
                preferred_element_type=F32,
            )
            results.append((tile_ref[e], both[:FIELDS] + both[FIELDS:]))
        for tile, value in results:
            out_ref[tile] = out_ref[tile] + value
        return 0

    lax.fori_loop(0, entries // SUB, group, 0)


def regrid_back(got, weights, slots, tile_ids, tiles):
    return pl.pallas_call(
        regrid_kernel,
        out_shape=jax.ShapeDtypeStruct((tiles, FIELDS, LANES), F32),
        in_specs=[spec_vmem(), spec_vmem(), spec_smem(), spec_smem()],
        out_specs=spec_vmem(),
        compiler_params=params(32),
        name="regrid_back",
    )(got, weights, slots, tile_ids)


def exchange(x):
    return lax.all_to_all(x, BOTH, split_axis=0, concat_axis=0, tiled=True)


def per_device(
    atm_state,
    diffusivity,
    surface_prev,
    flux_mix,
    entry_dest,
    entry_tile,
    entry_row,
    regrid_blocks,
    ocean_state,
    land_mask,
    flux_response,
):
    devices = lax.axis_size("sec") * lax.axis_size("tile")
    _, levels, columns = atm_state.shape
    blocks, tiles = levels // SUB, columns // LANES
    _, depth, rows, _ = ocean_state.shape

    a_tiles = atm_state.reshape(FIELDS, blocks, SUB, tiles, LANES).transpose(0, 1, 3, 2, 4)
    d_tiles = diffusivity.reshape(blocks, SUB, tiles, LANES).transpose(0, 2, 1, 3)
    s_tiles = surface_prev.reshape(FIELDS, tiles, LANES)
    y, e, outgoing = atm_forward(
        a_tiles, d_tiles, s_tiles, flux_mix, entry_dest, entry_tile, regrid_blocks, devices
    )

    q = ocean_state.reshape(FIELDS * depth, rows, LANES)
    outgoing, q = lax.optimization_barrier((outgoing, q))
    incoming = exchange(outgoing.reshape(devices, FLUXES * CAP, LANES))

    low_row, high_row, low_col, high_col, table, slots = ocean_edges(
        q, land_mask, entry_dest, entry_row, devices
    )
    edges = (
        lax.ppermute(low_row, "sec", shift("sec", -1)),
        lax.ppermute(high_row, "sec", shift("sec", 1)),
        lax.ppermute(low_col, "tile", shift("tile", -1)),
        lax.ppermute(high_col, "tile", shift("tile", 1)),
    )
    table = exchange(table)
    q_base, surf, bulk, hot, hot_t = ocean_step(q, land_mask, edges, table, flux_response, depth)

    q_next, returning = ocean_combine(
        incoming, hot, hot_t, bulk, surf, land_mask, flux_response, q_base, depth
    )
    returning, y, e = lax.optimization_barrier((returning, y, e))
    arrived = exchange(returning)
    atm_next = atm_back(y, e).transpose(0, 1, 3, 2, 4).reshape(FIELDS, levels, columns)
    back = regrid_back(
        arrived.reshape(devices * FIELDS * CAP, LANES), regrid_blocks, slots, entry_tile, tiles
    )
    surface_next = back.transpose(1, 0, 2).reshape(FIELDS, columns)
    return atm_next, q_next.reshape(ocean_state.shape), surface_next


def solution(mesh):
    return jax.shard_map(
        per_device,
        mesh=mesh,
        in_specs=(
            P(None, None, BOTH),
            P(None, BOTH),
            P(None, BOTH),
            P(),
            P(BOTH, None),
            P(BOTH),
            P(BOTH),
            P(BOTH, None, None),
            P(None, None, "sec", "tile"),
            P("sec", "tile"),
            P(),
        ),
        out_specs=(
            P(None, None, BOTH),
            P(None, None, "sec", "tile"),
            P(None, BOTH),
        ),
        check_vma=False,
    )
```

```python
import functools

import jax
import jax.numpy as jnp
from jax import lax
from jax.experimental import pallas as pl
from jax.experimental.pallas import tpu as pltpu
from jax.sharding import PartitionSpec as P

CAP = 4
LANES = 128
SUB = 8
FLUXES = 10
FEATURES = 12
FIELDS = 4
DIFFUSE = 0.2
CORIOLIS = 0.3
OCEAN_DT = 0.2
F32 = jnp.float32
BF16 = jnp.bfloat16
BOTH = ("sec", "tile")


def halves(x):
    high = x.astype(BF16)
    return high, (x - high.astype(F32)).astype(BF16)


def dot32(a, b):
    return jnp.dot(a, b, preferred_element_type=F32)


def spec_any():
    return pl.BlockSpec(memory_space=pltpu.HBM)


def spec_vmem():
    return pl.BlockSpec(memory_space=pltpu.VMEM)


def spec_smem():
    return pl.BlockSpec(memory_space=pltpu.SMEM)


def params(mib):
    return pltpu.CompilerParams(vmem_limit_bytes=mib * 2**20)


def atm_kernel(
    chunks,
    a_ref,
    d_ref,
    s_ref,
    mix_ref,
    dest_ref,
    tile_ref,
    row_ref,
    w_ref,
    y_ref,
    e_ref,
    out_ref,
    slot_ref,
    a_buf,
    d_buf,
    s_buf,
    w_buf,
    y_buf,
    e_buf,
    flux,
    count,
    in_sems,
    out_sems,
    s_sem,
    w_sem,
):
    blocks, tiles = a_buf.shape[1], a_buf.shape[2]
    levels = blocks * SUB
    entries = w_buf.shape[0]
    per = tiles // chunks
    groups = per // SUB
    devices = count.shape[0]
    chunk_rows = out_ref.shape[0] // devices
    table_rows = chunk_rows - FLUXES * CAP
    me = lax.axis_index("sec") * lax.axis_size("tile") + lax.axis_index("tile")

    def surface(v, tile):
        return s_buf[pl.ds(tile * FIELDS + v, SUB, stride=FIELDS), :]

    def loads(ci):
        at = pl.ds(ci * per, per)
        return (
            pltpu.make_async_copy(a_ref.at[:, :, at], a_buf.at[:, :, at], in_sems.at[ci, 0]),
            pltpu.make_async_copy(d_ref.at[:, at], d_buf.at[:, at], in_sems.at[ci, 1]),
        )

    def saves(ci):
        at = pl.ds(ci * per, per)
        return (
            pltpu.make_async_copy(y_buf.at[:, :, at], y_ref.at[:, :, at], out_sems.at[ci, 0]),
            pltpu.make_async_copy(e_buf.at[:, at], e_ref.at[:, at], out_sems.at[ci, 1]),
        )

    s_copy = pltpu.make_async_copy(s_ref, s_buf, s_sem)
    w_copy = pltpu.make_async_copy(w_ref, w_buf, w_sem)
    for copy in loads(0):
        copy.start()
    s_copy.start()
    for ci in range(1, chunks):
        for copy in loads(ci):
            copy.start()
    w_copy.start()

    a_rows = a_buf.reshape(FIELDS * blocks * tiles * SUB, LANES)
    d_rows = d_buf.reshape(blocks * tiles * SUB, LANES)
    s_copy.wait()
    for d in range(devices):
        count[d] = 0
    out_ref[...] = jnp.zeros_like(out_ref)

    def chunk(ci, _):
        for copy in loads(ci):
            copy.wait()
        first = ci * per

        def block(step, carry):
            lb = blocks - 1 - step
            bottom = jnp.where(lb == 0, 1.0, 0.0).astype(F32)
            carry = list(carry)
            for r in range(SUB - 1, -1, -1):
                for g in range(groups):
                    tile = first + g * SUB
                    grow, above, ys = carry[g]
                    coup = d_rows[pl.ds((lb * tiles + tile) * SUB + r, SUB, stride=SUB), :]
                    weight = 1.0 + above * grow
                    inverse = 1.0 / (weight + coup)
                    solved = []
                    for v in range(FIELDS):
                        row = ((v * blocks + lb) * tiles + tile) * SUB + r
                        rhs = a_rows[pl.ds(row, SUB, stride=SUB), :]
                        if r == 0:
                            rhs = rhs + coup * (surface(v, tile) * bottom)
                        value = (rhs + above * ys[v]) * inverse
                        y_buf[v, lb * SUB + r, pl.ds(tile, SUB), :] = value
                        solved.append(value)
                    e_buf[lb * SUB + r, pl.ds(tile, SUB), :] = coup * inverse
                    carry[g] = (weight * inverse, coup, tuple(solved))
            return tuple(carry)

        zero = jnp.zeros((SUB, LANES), F32)
        start = tuple((zero, zero, (zero,) * FIELDS) for _ in range(groups))
        final = lax.fori_loop(0, blocks, block, start)
        for copy in saves(ci):
            copy.start()
        for g in range(groups):
            tile = first + g * SUB
            _, coup, x0 = final[g]
            e1 = e_buf[1, pl.ds(tile, SUB), :]
            turb = [coup * (surface(v, tile) - x0[v]) for v in range(FIELDS)]
            x1 = [y_buf[v, 1, pl.ds(tile, SUB), :] + e1 * x0[v] for v in range(FIELDS)]
            feats = turb + list(x0) + [turb[v] * x1[v] for v in range(FIELDS)]
            for f in range(FLUXES):
                total = mix_ref[f, 0] * feats[0]
                for k in range(1, FEATURES):
                    total = total + mix_ref[f, k] * feats[k]
                flux[pl.ds(tile * 16 + f, SUB, stride=16), :] = total
        return 0

    lax.fori_loop(0, chunks, chunk, 0)
    w_copy.wait()

    spot = lax.broadcasted_iota(jnp.int32, (table_rows, LANES), 0) * LANES
    spot = spot + lax.broadcasted_iota(jnp.int32, (table_rows, LANES), 1)

    def entry(e, _):
        d = dest_ref[e]
        k = count[d]
        count[d] = k + 1
        slot_ref[e] = d * (FIELDS * CAP) + k
        here = me * (2 * CAP) + k
        hit = (spot == here) | (spot == here + CAP)
        table = pl.ds(d * chunk_rows + FLUXES * CAP, table_rows)
        out_ref[table, :] += jnp.where(hit, row_ref[e] + 1, 0).astype(F32)
        picked = flux[pl.ds(pl.multiple_of(tile_ref[e] * 16, 16), 16), :]
        high, low = halves(picked)
        both = dot32(jnp.concatenate([high, low], axis=0), w_buf[e])
        both = both[:16] + both[16:]
        row = d * chunk_rows + k
        out_ref[pl.ds(row, SUB, stride=CAP), :] = both[:SUB]
        out_ref[pl.ds(row + SUB * CAP, FLUXES - SUB, stride=CAP), :] = both[SUB:FLUXES]
        return 0

    lax.fori_loop(0, entries, entry, 0, unroll=8)
    for ci in range(chunks):
        for copy in saves(ci):
            copy.wait()


def atm_forward(a_tiles, d_tiles, s_rows, mix, dest, tile_ids, row_ids, weights, devices):
    _, blocks, tiles, _, _ = a_tiles.shape
    levels = blocks * SUB
    entries = weights.shape[0]
    chunks = 2
    chunk_rows = FLUXES * CAP + devices * 2 * CAP // LANES
    return pl.pallas_call(
        functools.partial(atm_kernel, chunks),
        out_shape=(
            jax.ShapeDtypeStruct((FIELDS, levels, tiles, LANES), F32),
            jax.ShapeDtypeStruct((levels, tiles, LANES), F32),
            jax.ShapeDtypeStruct((devices * chunk_rows, LANES), F32),
            jax.ShapeDtypeStruct((entries,), jnp.int32),
        ),
        in_specs=[
            spec_any(),
            spec_any(),
            spec_any(),
            spec_smem(),
            spec_smem(),
            spec_smem(),
            spec_smem(),
            spec_any(),
        ],
        out_specs=(spec_any(), spec_any(), spec_vmem(), spec_smem()),
        scratch_shapes=[
            pltpu.VMEM(a_tiles.shape, F32),
            pltpu.VMEM(d_tiles.shape, F32),
            pltpu.VMEM(s_rows.shape, F32),
            pltpu.VMEM(weights.shape, BF16),
            pltpu.VMEM((FIELDS, levels, tiles, LANES), F32),
            pltpu.VMEM((levels, tiles, LANES), F32),
            pltpu.VMEM((tiles * 16, LANES), F32),
            pltpu.SMEM((devices,), jnp.int32),
            pltpu.SemaphoreType.DMA((chunks, 2)),
            pltpu.SemaphoreType.DMA((chunks, 2)),
            pltpu.SemaphoreType.DMA,
            pltpu.SemaphoreType.DMA,
        ],
        compiler_params=params(60),
        name="atm_forward",
    )(a_tiles, d_tiles, s_rows, mix, dest, tile_ids, row_ids, weights)


def back_kernel(y_ref, e_ref, out_ref):
    blocks, tiles = out_ref.shape[1], out_ref.shape[2]
    rows = out_ref.reshape(FIELDS * blocks * tiles * SUB, LANES)
    groups = tiles // SUB

    def block(lb, carry):
        carry = list(carry)
        for r in range(SUB):
            for g in range(groups):
                coef = e_ref[lb * SUB + r, pl.ds(g * SUB, SUB), :]
                if r == 0:
                    coef = coef * jnp.where(lb == 0, 0.0, 1.0).astype(F32)
                for v in range(FIELDS):
                    x = y_ref[v, lb * SUB + r, pl.ds(g * SUB, SUB), :]
                    x = x + coef * carry[g * FIELDS + v]
                    row = ((v * blocks + lb) * tiles + g * SUB) * SUB + r
                    rows[pl.ds(row, SUB, stride=SUB), :] = x
                    carry[g * FIELDS + v] = x
        return tuple(carry)

    zero = jnp.zeros((SUB, LANES), F32)
    lax.fori_loop(0, blocks, block, (zero,) * (groups * FIELDS))


def atm_back(y, e):
    _, levels, tiles, _ = y.shape
    blocks = levels // SUB
    per = 16
    return pl.pallas_call(
        back_kernel,
        grid=(tiles // per,),
        out_shape=jax.ShapeDtypeStruct((FIELDS, blocks, tiles, SUB, LANES), F32),
        in_specs=[
            pl.BlockSpec((FIELDS, levels, per, LANES), lambda i: (0, 0, i, 0)),
            pl.BlockSpec((levels, per, LANES), lambda i: (0, i, 0)),
        ],
        out_specs=pl.BlockSpec((FIELDS, blocks, per, SUB, LANES), lambda i: (0, 0, i, 0, 0)),
        compiler_params=params(56),
        cost_estimate=pl.CostEstimate(
            flops=2 * y.size, bytes_accessed=9 * y.size, transcendentals=0
        ),
        name="atm_back",
    )(y, e)


def edge_kernel(q_ref, m_ref, low_row, high_row, low_col, high_col):
    fields, rows, _ = q_ref.shape
    mask = m_ref[...].astype(F32)
    for dst, at in ((low_row, 0), (high_row, rows - 1)):
        dst[...] = jnp.zeros_like(dst)
        for i in range(fields):
            dst[i : i + 1, :] = q_ref[i, at : at + 1, :]
        dst[fields : fields + 1, :] = mask[at : at + 1, :]

    lane = lax.broadcasted_iota(jnp.int32, (rows, LANES), 1)
    low = jnp.zeros((rows, LANES), F32)
    high = jnp.zeros((rows, LANES), F32)
    for i in range(fields + 1):
        cells = q_ref[i] if i < fields else mask
        turned = pltpu.roll(cells, i, 1) if i else cells
        low = jnp.where(lane == i, turned, low)
        high = jnp.where(lane == (i + LANES - 1) % LANES, turned, high)
    low_col[...] = low
    high_col[...] = high


def ocean_edges(q, mask):
    pad = -(-(q.shape[0] + 1) // SUB) * SUB
    row = jax.ShapeDtypeStruct((pad, LANES), F32)
    col = jax.ShapeDtypeStruct(mask.shape, F32)
    return pl.pallas_call(
        edge_kernel,
        out_shape=(row, row, col, col),
        in_specs=[spec_vmem(), spec_vmem()],
        out_specs=(spec_vmem(),) * 4,
        compiler_params=params(32),
        cost_estimate=pl.CostEstimate(flops=q.size, bytes_accessed=4 * q.size, transcendentals=0),
        name="ocean_edges",
    )(q, mask)


def shift(axis, step):
    count = lax.axis_size(axis)
    if step > 0:
        return [(i, i + 1) for i in range(count - 1)]
    return [(i + 1, i) for i in range(count - 1)]


def ocean_kernel(
    depth,
    q_ref,
    m_ref,
    east_ref,
    west_ref,
    north_ref,
    south_ref,
    resp_ref,
    out_ref,
    surf_ref,
    bulk_ref,
):
    fields, rows, _ = q_ref.shape
    lane = lax.broadcasted_iota(jnp.int32, (rows, LANES), 1)
    last, first = lane == LANES - 1, lane == 0

    def south_at(i):
        return (i + LANES - 1) % LANES

    def around(cells, i):
        east = jnp.concatenate([cells[1:], east_ref[i : i + 1, :]], axis=0)
        west = jnp.concatenate([west_ref[i : i + 1, :], cells[:-1]], axis=0)
        north = jnp.where(last, north_ref[:, i : i + 1], pltpu.roll(cells, LANES - 1, 1))
        south = jnp.where(first, south_ref[:, south_at(i) : south_at(i) + 1], pltpu.roll(cells, 1, 1))
        return east, west, north, south

    mask = m_ref[...].astype(F32)
    m_east, m_west, m_north, m_south = around(mask, fields)
    m_all = m_east + m_west + m_north + m_south
    for level in range(depth):
        zonal = q_ref[2 * depth + level]
        merid = q_ref[3 * depth + level]
        for v in range(FIELDS):
            i = v * depth + level
            cells = q_ref[i]
            east, west, north, south = around(cells, i)
            lap = m_east * east + m_west * west + m_north * north + m_south * south
            lap = lap - m_all * cells
            adv = 0.5 * (zonal * (east - west) + merid * (north - south))
            tend = DIFFUSE * lap - adv
            if v == 2:
                tend = tend + CORIOLIS * merid
            if v == 3:
                tend = tend - CORIOLIS * zonal
            value = mask * (cells + OCEAN_DT * tend)
            out_ref[i] = value
            if level == 0:
                surf_ref[v] = value

    tops = [q_ref[v * depth] for v in range(FIELDS)]
    for f in range(FLUXES):
        total = resp_ref[0, f] * tops[0]
        for v in range(1, FIELDS):
            total = total + resp_ref[v, f] * tops[v]
        bulk_ref[f] = 1.0 + 0.5 * jnp.tanh(total)


def ocean_step(q, mask, edges, response, depth):
    rows = q.shape[1]
    return pl.pallas_call(
        functools.partial(ocean_kernel, depth),
        out_shape=(
            jax.ShapeDtypeStruct(q.shape, F32),
            jax.ShapeDtypeStruct((FIELDS, rows, LANES), F32),
            jax.ShapeDtypeStruct((FLUXES, rows, LANES), F32),
        ),
        in_specs=[spec_vmem()] * 6 + [spec_smem()],
        out_specs=(spec_vmem(),) * 3,
        compiler_params=params(32),
        cost_estimate=pl.CostEstimate(
            flops=30 * q.size, bytes_accessed=8 * q.size, transcendentals=0
        ),
        name="ocean_step",
    )(q, mask, *edges, response)


def combine_kernel(
    depth, got_ref, bulk_ref, surf_ref, m_ref, resp_ref, q_ref, out_ref, back_ref, top, sems
):
    rows = m_ref.shape[0]
    sources = back_ref.shape[0]
    chunk_rows = got_ref.shape[0] // sources
    table_rows = chunk_rows - FLUXES * CAP

    x = lax.broadcasted_iota(jnp.int32, (2 * rows, LANES), 0)
    spot = lax.broadcasted_iota(jnp.int32, (2 * rows, LANES), 1)
    pair = (spot // CAP) % 2 == x // rows
    wanted = jnp.where(pair, (x % rows + 1).astype(F32), -1.0)
    hots = []
    for j in range(table_rows):
        seen = got_ref[pl.ds(FLUXES * CAP + j, sources, stride=chunk_rows), :]
        seen = jnp.sum(seen, axis=0, keepdims=True)
        hots.append((seen == wanted).astype(F32))
    hot = jnp.concatenate([h.astype(BF16) for h in hots], axis=1)

    force = [None] * FIELDS
    for j in range(FLUXES // 2):
        data = jnp.concatenate(
            [got_ref[pl.ds(s * chunk_rows + j * SUB, SUB), :] for s in range(sources)], axis=0
        )
        high, low = halves(data)
        both = dot32(hot, high) + dot32(hot, low)
        for p in range(2):
            f = 2 * j + p
            drive = both[p * rows : (p + 1) * rows] * bulk_ref[f]
            for g in range(FIELDS):
                term = resp_ref[g, f] * drive
                force[g] = term if f == 0 else force[g] + term
    mask = m_ref[...].astype(F32)
    for g in range(FIELDS):
        top[g] = surf_ref[g] + mask * force[g]
    copies = [
        pltpu.make_async_copy(top.at[g], out_ref.at[g * depth], sems.at[g]) for g in range(FIELDS)
    ]
    for copy in copies:
        copy.start()
    hot_t = jnp.concatenate([jnp.transpose(h).astype(BF16) for h in hots], axis=0)
    for j in range(FIELDS // 2):
        pair = jnp.concatenate([top[2 * j], top[2 * j + 1]], axis=0)
        high, low = halves(pair)
        both = dot32(hot_t, high) + dot32(hot_t, low)
        back_ref[:, j * SUB : (j + 1) * SUB, :] = both.reshape(sources, SUB, LANES)
    for copy in copies:
        copy.wait()


def ocean_combine(got, bulk, surf, mask, response, q_next, depth, sources):
    return pl.pallas_call(
        functools.partial(combine_kernel, depth),
        out_shape=(
            jax.ShapeDtypeStruct(q_next.shape, F32),
            jax.ShapeDtypeStruct((sources, FIELDS * CAP, LANES), F32),
        ),
        in_specs=[spec_vmem()] * 4 + [spec_smem(), spec_any()],
        out_specs=(spec_any(), spec_vmem()),
        scratch_shapes=[
            pltpu.VMEM(surf.shape, F32),
            pltpu.SemaphoreType.DMA((FIELDS,)),
        ],
        input_output_aliases={5: 0},
        compiler_params=params(32),
        name="ocean_combine",
    )(got, bulk, surf, mask, response, q_next)


def regrid_kernel(got_ref, w_ref, slot_ref, tile_ref, out_ref):
    entries = w_ref.shape[0]
    out_ref[...] = jnp.zeros_like(out_ref)

    def group(i, _):
        results = []
        for u in range(SUB):
            e = i * SUB + u
            slot = slot_ref[e]
            rows = got_ref[pl.ds(slot, FIELDS, stride=CAP), :]
            high, low = halves(rows)
            both = lax.dot_general(
                jnp.concatenate([high, low], axis=0),
                w_ref[e],
                (((1,), (1,)), ((), ())),
                preferred_element_type=F32,
            )
            results.append((tile_ref[e], both[:FIELDS] + both[FIELDS:]))
        for tile, value in results:
            out_ref[tile] = out_ref[tile] + value
        return 0

    lax.fori_loop(0, entries // SUB, group, 0)


def regrid_back(got, weights, slots, tile_ids, tiles):
    return pl.pallas_call(
        regrid_kernel,
        out_shape=jax.ShapeDtypeStruct((tiles, FIELDS, LANES), F32),
        in_specs=[spec_vmem(), spec_vmem(), spec_smem(), spec_smem()],
        out_specs=spec_vmem(),
        compiler_params=params(32),
        name="regrid_back",
    )(got, weights, slots, tile_ids)


def exchange(x):
    return lax.all_to_all(x, BOTH, split_axis=0, concat_axis=0, tiled=True)


def per_device(
    atm_state,
    diffusivity,
    surface_prev,
    flux_mix,
    entry_dest,
    entry_tile,
    entry_row,
    regrid_blocks,
    ocean_state,
    land_mask,
    flux_response,
):
    devices = lax.axis_size("sec") * lax.axis_size("tile")
    _, levels, columns = atm_state.shape
    blocks, tiles = levels // SUB, columns // LANES
    _, depth, rows, _ = ocean_state.shape

    a_tiles = atm_state.reshape(FIELDS, blocks, SUB, tiles, LANES).transpose(0, 1, 3, 2, 4)
    d_tiles = diffusivity.reshape(blocks, SUB, tiles, LANES).transpose(0, 2, 1, 3)
    s_rows = surface_prev.reshape(FIELDS, tiles, LANES).transpose(1, 0, 2)
    s_rows = s_rows.reshape(tiles * FIELDS, LANES)
    y, e, outgoing, slots = atm_forward(
        a_tiles,
        d_tiles,
        s_rows,
        flux_mix,
        entry_dest[:, 0],
        entry_tile,
        entry_row,
        regrid_blocks,
        devices,
    )

    q = ocean_state.reshape(FIELDS * depth, rows, LANES)
    outgoing, q = lax.optimization_barrier((outgoing, q))
    chunk_rows = outgoing.shape[0] // devices
    incoming = exchange(outgoing.reshape(devices, chunk_rows // 2, 2, LANES))
    incoming = incoming.reshape(outgoing.shape)

    low_row, high_row, low_col, high_col = ocean_edges(q, land_mask)
    edges = (
        lax.ppermute(low_row, "sec", shift("sec", -1)),
        lax.ppermute(high_row, "sec", shift("sec", 1)),
        lax.ppermute(low_col, "tile", shift("tile", -1)),
        lax.ppermute(high_col, "tile", shift("tile", 1)),
    )
    q_base, surf, bulk = ocean_step(q, land_mask, edges, flux_response, depth)

    q_next, returning = ocean_combine(
        incoming, bulk, surf, land_mask, flux_response, q_base, depth, devices
    )
    returning, y, e = lax.optimization_barrier((returning, y, e))
    arrived = exchange(returning)
    atm_next = atm_back(y, e).transpose(0, 1, 3, 2, 4).reshape(FIELDS, levels, columns)
    back = regrid_back(
        arrived.reshape(devices * FIELDS * CAP, LANES), regrid_blocks, slots, entry_tile, tiles
    )
    surface_next = back.transpose(1, 0, 2).reshape(FIELDS, columns)
    return atm_next, q_next.reshape(ocean_state.shape), surface_next


def solution(mesh):
    return jax.shard_map(
        per_device,
        mesh=mesh,
        in_specs=(
            P(None, None, BOTH),
            P(None, BOTH),
            P(None, BOTH),
            P(),
            P(BOTH, None),
            P(BOTH),
            P(BOTH),
            P(BOTH, None, None),
            P(None, None, "sec", "tile"),
            P("sec", "tile"),
            P(),
        ),
        out_specs=(
            P(None, None, BOTH),
            P(None, None, "sec", "tile"),
            P(None, BOTH),
        ),
        check_vma=False,
    )
```

```python
import functools

import jax
import jax.numpy as jnp
from jax import lax
from jax.experimental import pallas as pl
from jax.experimental.pallas import tpu as pltpu
from jax.sharding import PartitionSpec as P

CAP = 4
LANES = 128
SUB = 8
FLUXES = 10
FEATURES = 12
FIELDS = 4
DIFFUSE = 0.2
CORIOLIS = 0.3
OCEAN_DT = 0.2
F32 = jnp.float32
BF16 = jnp.bfloat16
BOTH = ("sec", "tile")


def halves(x):
    high = x.astype(BF16)
    return high, (x - high.astype(F32)).astype(BF16)


def dot32(a, b):
    return jnp.dot(a, b, preferred_element_type=F32)


def spec_any():
    return pl.BlockSpec(memory_space=pltpu.HBM)


def spec_vmem():
    return pl.BlockSpec(memory_space=pltpu.VMEM)


def spec_smem():
    return pl.BlockSpec(memory_space=pltpu.SMEM)


def params(mib):
    return pltpu.CompilerParams(vmem_limit_bytes=mib * 2**20)


def atm_kernel(
    chunks,
    a_ref,
    d_ref,
    s_ref,
    mix_ref,
    dest_ref,
    tile_ref,
    row_ref,
    w_ref,
    y_ref,
    e_ref,
    out_ref,
    slot_ref,
    a_buf,
    d_buf,
    s_buf,
    w_buf,
    y_buf,
    e_buf,
    flux,
    count,
    in_sems,
    out_sems,
    s_sem,
    w_sem,
):
    blocks, tiles = a_buf.shape[1], a_buf.shape[2]
    levels = blocks * SUB
    entries = w_buf.shape[0]
    per = tiles // chunks
    groups = per // SUB
    devices = count.shape[0]
    chunk_rows = out_ref.shape[0] // devices
    table_rows = chunk_rows - FLUXES * CAP
    me = lax.axis_index("sec") * lax.axis_size("tile") + lax.axis_index("tile")

    def surface(v, tile):
        return s_buf[pl.ds(tile * FIELDS + v, SUB, stride=FIELDS), :]

    def loads(ci):
        at = pl.ds(ci * per, per)
        return (
            pltpu.make_async_copy(a_ref.at[:, :, at], a_buf.at[:, :, at], in_sems.at[ci, 0]),
            pltpu.make_async_copy(d_ref.at[:, at], d_buf.at[:, at], in_sems.at[ci, 1]),
        )

    def saves(ci):
        at = pl.ds(ci * per, per)
        return (
            pltpu.make_async_copy(y_buf.at[:, :, at], y_ref.at[:, :, at], out_sems.at[ci, 0]),
            pltpu.make_async_copy(e_buf.at[:, at], e_ref.at[:, at], out_sems.at[ci, 1]),
        )

    s_copy = pltpu.make_async_copy(s_ref, s_buf, s_sem)
    w_copy = pltpu.make_async_copy(w_ref, w_buf, w_sem)
    for copy in loads(0):
        copy.start()
    s_copy.start()
    for ci in range(1, chunks):
        for copy in loads(ci):
            copy.start()
    w_copy.start()

    a_rows = a_buf.reshape(FIELDS * blocks * tiles * SUB, LANES)
    d_rows = d_buf.reshape(blocks * tiles * SUB, LANES)
    s_copy.wait()
    for d in range(devices):
        count[d] = 0
    out_ref[...] = jnp.zeros_like(out_ref)

    def chunk(ci, _):
        for copy in loads(ci):
            copy.wait()
        first = ci * per

        def block(step, carry):
            lb = blocks - 1 - step
            bottom = jnp.where(lb == 0, 1.0, 0.0).astype(F32)
            carry = list(carry)
            for r in range(SUB - 1, -1, -1):
                for g in range(groups):
                    tile = first + g * SUB
                    grow, above, ys = carry[g]
                    coup = d_rows[pl.ds((lb * tiles + tile) * SUB + r, SUB, stride=SUB), :]
                    weight = 1.0 + above * grow
                    inverse = 1.0 / (weight + coup)
                    solved = []
                    for v in range(FIELDS):
                        row = ((v * blocks + lb) * tiles + tile) * SUB + r
                        rhs = a_rows[pl.ds(row, SUB, stride=SUB), :]
                        if r == 0:
                            rhs = rhs + coup * (surface(v, tile) * bottom)
                        value = (rhs + above * ys[v]) * inverse
                        y_buf[v, lb * SUB + r, pl.ds(tile, SUB), :] = value
                        solved.append(value)
                    e_buf[lb * SUB + r, pl.ds(tile, SUB), :] = coup * inverse
                    carry[g] = (weight * inverse, coup, tuple(solved))
            return tuple(carry)

        zero = jnp.zeros((SUB, LANES), F32)
        start = tuple((zero, zero, (zero,) * FIELDS) for _ in range(groups))
        final = lax.fori_loop(0, blocks, block, start)
        for copy in saves(ci):
            copy.start()
        for g in range(groups):
            tile = first + g * SUB
            _, coup, x0 = final[g]
            e1 = e_buf[1, pl.ds(tile, SUB), :]
            turb = [coup * (surface(v, tile) - x0[v]) for v in range(FIELDS)]
            x1 = [y_buf[v, 1, pl.ds(tile, SUB), :] + e1 * x0[v] for v in range(FIELDS)]
            feats = turb + list(x0) + [turb[v] * x1[v] for v in range(FIELDS)]
            for f in range(FLUXES):
                total = mix_ref[f, 0] * feats[0]
                for k in range(1, FEATURES):
                    total = total + mix_ref[f, k] * feats[k]
                flux[pl.ds(tile * 16 + f, SUB, stride=16), :] = total
        return 0

    lax.fori_loop(0, chunks, chunk, 0)
    w_copy.wait()

    spot = lax.broadcasted_iota(jnp.int32, (table_rows, LANES), 0) * LANES
    spot = spot + lax.broadcasted_iota(jnp.int32, (table_rows, LANES), 1)

    def entry(e, _):
        d = dest_ref[e]
        k = count[d]
        count[d] = k + 1
        slot_ref[e] = d * (FIELDS * CAP) + k
        here = me * (2 * CAP) + k
        hit = (spot == here) | (spot == here + CAP)
        table = pl.ds(d * chunk_rows + FLUXES * CAP, table_rows)
        out_ref[table, :] += jnp.where(hit, row_ref[e] + 1, 0).astype(F32)
        picked = flux[pl.ds(pl.multiple_of(tile_ref[e] * 16, 16), 16), :]
        high, low = halves(picked)
        both = dot32(jnp.concatenate([high, low], axis=0), w_buf[e])
        both = both[:16] + both[16:]
        row = d * chunk_rows + k
        out_ref[pl.ds(row, SUB, stride=CAP), :] = both[:SUB]
        out_ref[pl.ds(row + SUB * CAP, FLUXES - SUB, stride=CAP), :] = both[SUB:FLUXES]
        return 0

    lax.fori_loop(0, entries, entry, 0, unroll=8)
    for ci in range(chunks):
        for copy in saves(ci):
            copy.wait()


def atm_forward(a_tiles, d_tiles, s_rows, mix, dest, tile_ids, row_ids, weights, devices):
    _, blocks, tiles, _, _ = a_tiles.shape
    levels = blocks * SUB
    entries = weights.shape[0]
    chunks = 2
    chunk_rows = FLUXES * CAP + devices * 2 * CAP // LANES
    return pl.pallas_call(
        functools.partial(atm_kernel, chunks),
        out_shape=(
            jax.ShapeDtypeStruct((FIELDS, levels, tiles, LANES), F32),
            jax.ShapeDtypeStruct((levels, tiles, LANES), F32),
            jax.ShapeDtypeStruct((devices * chunk_rows, LANES), F32),
            jax.ShapeDtypeStruct((entries,), jnp.int32),
        ),
        in_specs=[
            spec_any(),
            spec_any(),
            spec_any(),
            spec_smem(),
            spec_smem(),
            spec_smem(),
            spec_smem(),
            spec_any(),
        ],
        out_specs=(spec_any(), spec_any(), spec_vmem(), spec_smem()),
        scratch_shapes=[
            pltpu.VMEM(a_tiles.shape, F32),
            pltpu.VMEM(d_tiles.shape, F32),
            pltpu.VMEM(s_rows.shape, F32),
            pltpu.VMEM(weights.shape, BF16),
            pltpu.VMEM((FIELDS, levels, tiles, LANES), F32),
            pltpu.VMEM((levels, tiles, LANES), F32),
            pltpu.VMEM((tiles * 16, LANES), F32),
            pltpu.SMEM((devices,), jnp.int32),
            pltpu.SemaphoreType.DMA((chunks, 2)),
            pltpu.SemaphoreType.DMA((chunks, 2)),
            pltpu.SemaphoreType.DMA,
            pltpu.SemaphoreType.DMA,
        ],
        compiler_params=params(60),
        name="atm_forward",
    )(a_tiles, d_tiles, s_rows, mix, dest, tile_ids, row_ids, weights)


def back_kernel(y_ref, e_ref, out_ref):
    blocks, tiles = out_ref.shape[1], out_ref.shape[2]
    rows = out_ref.reshape(FIELDS * blocks * tiles * SUB, LANES)
    groups = tiles // SUB

    def block(lb, carry):
        carry = list(carry)
        for r in range(SUB):
            for g in range(groups):
                coef = e_ref[lb * SUB + r, pl.ds(g * SUB, SUB), :]
                if r == 0:
                    coef = coef * jnp.where(lb == 0, 0.0, 1.0).astype(F32)
                for v in range(FIELDS):
                    x = y_ref[v, lb * SUB + r, pl.ds(g * SUB, SUB), :]
                    x = x + coef * carry[g * FIELDS + v]
                    row = ((v * blocks + lb) * tiles + g * SUB) * SUB + r
                    rows[pl.ds(row, SUB, stride=SUB), :] = x
                    carry[g * FIELDS + v] = x
        return tuple(carry)

    zero = jnp.zeros((SUB, LANES), F32)
    lax.fori_loop(0, blocks, block, (zero,) * (groups * FIELDS))


def atm_back(y, e):
    _, levels, tiles, _ = y.shape
    blocks = levels // SUB
    per = 16
    return pl.pallas_call(
        back_kernel,
        grid=(tiles // per,),
        out_shape=jax.ShapeDtypeStruct((FIELDS, blocks, tiles, SUB, LANES), F32),
        in_specs=[
            pl.BlockSpec((FIELDS, levels, per, LANES), lambda i: (0, 0, i, 0)),
            pl.BlockSpec((levels, per, LANES), lambda i: (0, i, 0)),
        ],
        out_specs=pl.BlockSpec((FIELDS, blocks, per, SUB, LANES), lambda i: (0, 0, i, 0, 0)),
        compiler_params=params(16),
        cost_estimate=pl.CostEstimate(
            flops=2 * y.size, bytes_accessed=9 * y.size, transcendentals=0
        ),
        name="atm_back",
    )(y, e)


def edge_kernel(q_ref, m_ref, low_row, high_row, low_col, high_col):
    fields, rows, _ = q_ref.shape
    mask = m_ref[...].astype(F32)
    for dst, at in ((low_row, 0), (high_row, rows - 1)):
        dst[...] = jnp.zeros_like(dst)
        for i in range(fields):
            dst[i : i + 1, :] = q_ref[i, at : at + 1, :]
        dst[fields : fields + 1, :] = mask[at : at + 1, :]

    lane = lax.broadcasted_iota(jnp.int32, (rows, LANES), 1)
    low = jnp.zeros((rows, LANES), F32)
    high = jnp.zeros((rows, LANES), F32)
    for i in range(fields + 1):
        cells = q_ref[i] if i < fields else mask
        turned = pltpu.roll(cells, i, 1) if i else cells
        low = jnp.where(lane == i, turned, low)
        high = jnp.where(lane == (i + LANES - 1) % LANES, turned, high)
    low_col[...] = low
    high_col[...] = high


def ocean_edges(q, mask):
    pad = -(-(q.shape[0] + 1) // SUB) * SUB
    row = jax.ShapeDtypeStruct((pad, LANES), F32)
    col = jax.ShapeDtypeStruct(mask.shape, F32)
    return pl.pallas_call(
        edge_kernel,
        out_shape=(row, row, col, col),
        in_specs=[spec_vmem(), spec_vmem()],
        out_specs=(spec_vmem(),) * 4,
        compiler_params=params(8),
        cost_estimate=pl.CostEstimate(flops=q.size, bytes_accessed=4 * q.size, transcendentals=0),
        name="ocean_edges",
    )(q, mask)


def shift(axis, step):
    count = lax.axis_size(axis)
    if step > 0:
        return [(i, i + 1) for i in range(count - 1)]
    return [(i + 1, i) for i in range(count - 1)]


def bulk_kernel(q_ref, resp_ref, bulk_ref):
    depth = q_ref.shape[0] // FIELDS
    tops = [q_ref[v * depth] for v in range(FIELDS)]
    for f in range(FLUXES):
        total = resp_ref[0, f] * tops[0]
        for v in range(1, FIELDS):
            total = total + resp_ref[v, f] * tops[v]
        bulk_ref[f] = 1.0 + 0.5 * jnp.tanh(total)


def ocean_bulk(q, response):
    return pl.pallas_call(
        bulk_kernel,
        out_shape=jax.ShapeDtypeStruct((FLUXES,) + q.shape[1:], F32),
        in_specs=[spec_vmem(), spec_smem()],
        out_specs=spec_vmem(),
        compiler_params=params(8),
        cost_estimate=pl.CostEstimate(
            flops=3 * q.size, bytes_accessed=2 * q.size, transcendentals=q.size // 3
        ),
        name="ocean_bulk",
    )(q, response)


def stencil(levels, q_ref, m_ref, east_ref, west_ref, north_ref, south_ref, save):
    fields, rows, _ = q_ref.shape
    depth = fields // FIELDS
    lane = lax.broadcasted_iota(jnp.int32, (rows, LANES), 1)
    last, first = lane == LANES - 1, lane == 0

    def around(cells, i):
        high = (i + LANES - 1) % LANES
        east = jnp.concatenate([cells[1:], east_ref[i : i + 1, :]], axis=0)
        west = jnp.concatenate([west_ref[i : i + 1, :], cells[:-1]], axis=0)
        north = jnp.where(last, north_ref[:, i : i + 1], pltpu.roll(cells, LANES - 1, 1))
        south = jnp.where(first, south_ref[:, high : high + 1], pltpu.roll(cells, 1, 1))
        return east, west, north, south

    mask = m_ref[...].astype(F32)
    m_east, m_west, m_north, m_south = around(mask, fields)
    m_all = m_east + m_west + m_north + m_south
    for level in levels:
        zonal = q_ref[2 * depth + level]
        merid = q_ref[3 * depth + level]
        for v in range(FIELDS):
            i = v * depth + level
            cells = q_ref[i]
            east, west, north, south = around(cells, i)
            lap = m_east * east + m_west * west + m_north * north + m_south * south
            lap = lap - m_all * cells
            adv = 0.5 * (zonal * (east - west) + merid * (north - south))
            tend = DIFFUSE * lap - adv
            if v == 2:
                tend = tend + CORIOLIS * merid
            if v == 3:
                tend = tend - CORIOLIS * zonal
            save(v, level, mask * (cells + OCEAN_DT * tend))


def top_kernel(q_ref, m_ref, east_ref, west_ref, north_ref, south_ref, surf_ref):
    def save(v, level, value):
        surf_ref[v] = value

    stencil((0,), q_ref, m_ref, east_ref, west_ref, north_ref, south_ref, save)


def ocean_top(q, mask, edges):
    return pl.pallas_call(
        top_kernel,
        out_shape=jax.ShapeDtypeStruct((FIELDS,) + q.shape[1:], F32),
        in_specs=[spec_vmem()] * 6,
        out_specs=spec_vmem(),
        compiler_params=params(8),
        cost_estimate=pl.CostEstimate(flops=4 * q.size, bytes_accessed=q.size, transcendentals=0),
        name="ocean_top",
    )(q, mask, *edges)


def deep_kernel(q_ref, m_ref, east_ref, west_ref, north_ref, south_ref, top_ref, out_ref):
    depth = q_ref.shape[0] // FIELDS

    def save(v, level, value):
        out_ref[v * depth + level] = value

    for v in range(FIELDS):
        out_ref[v * depth] = top_ref[v]
    levels = range(1, depth)
    stencil(levels, q_ref, m_ref, east_ref, west_ref, north_ref, south_ref, save)


def ocean_deep(q, mask, edges, top):
    return pl.pallas_call(
        deep_kernel,
        out_shape=jax.ShapeDtypeStruct(q.shape, F32),
        in_specs=[spec_vmem()] * 7,
        out_specs=spec_vmem(),
        compiler_params=params(8),
        cost_estimate=pl.CostEstimate(
            flops=30 * q.size, bytes_accessed=8 * q.size, transcendentals=0
        ),
        name="ocean_deep",
    )(q, mask, *edges, top)


def combine_kernel(
    got_ref, bulk_ref, surf_ref, m_ref, resp_ref, top, back_ref
):
    rows = m_ref.shape[0]
    sources = back_ref.shape[0]
    chunk_rows = got_ref.shape[0] // sources
    table_rows = chunk_rows - FLUXES * CAP

    x = lax.broadcasted_iota(jnp.int32, (2 * rows, LANES), 0)
    spot = lax.broadcasted_iota(jnp.int32, (2 * rows, LANES), 1)
    pair = (spot // CAP) % 2 == x // rows
    wanted = jnp.where(pair, (x % rows + 1).astype(F32), -1.0)
    hots = []
    for j in range(table_rows):
        seen = got_ref[pl.ds(FLUXES * CAP + j, sources, stride=chunk_rows), :]
        seen = jnp.sum(seen, axis=0, keepdims=True)
        hots.append((seen == wanted).astype(F32))
    hot = jnp.concatenate([h.astype(BF16) for h in hots], axis=1)

    force = [None] * FIELDS
    for j in range(FLUXES // 2):
        data = jnp.concatenate(
            [got_ref[pl.ds(s * chunk_rows + j * SUB, SUB), :] for s in range(sources)], axis=0
        )
        high, low = halves(data)
        both = dot32(hot, high) + dot32(hot, low)
        for p in range(2):
            f = 2 * j + p
            drive = both[p * rows : (p + 1) * rows] * bulk_ref[f]
            for g in range(FIELDS):
                term = resp_ref[g, f] * drive
                force[g] = term if f == 0 else force[g] + term
    mask = m_ref[...].astype(F32)
    for g in range(FIELDS):
        top[g] = surf_ref[g] + mask * force[g]
    hot_t = jnp.concatenate([jnp.transpose(h).astype(BF16) for h in hots], axis=0)
    for j in range(FIELDS // 2):
        pair = jnp.concatenate([top[2 * j], top[2 * j + 1]], axis=0)
        high, low = halves(pair)
        both = dot32(hot_t, high) + dot32(hot_t, low)
        back_ref[:, j * SUB : (j + 1) * SUB, :] = both.reshape(sources, SUB, LANES)


def ocean_combine(got, bulk, surf, mask, response, sources):
    return pl.pallas_call(
        combine_kernel,
        out_shape=(
            jax.ShapeDtypeStruct(surf.shape, F32),
            jax.ShapeDtypeStruct((sources, FIELDS * CAP, LANES), F32),
        ),
        in_specs=[spec_vmem()] * 4 + [spec_smem()],
        out_specs=(spec_vmem(), spec_vmem()),
        compiler_params=params(16),
        cost_estimate=pl.CostEstimate(
            flops=4 * got.size, bytes_accessed=4 * got.size, transcendentals=0
        ),
        name="ocean_combine",
    )(got, bulk, surf, mask, response)


def regrid_kernel(got_ref, w_ref, slot_ref, tile_ref, out_ref):
    entries = w_ref.shape[0]
    out_ref[...] = jnp.zeros_like(out_ref)

    def group(i, _):
        results = []
        for u in range(SUB):
            e = i * SUB + u
            slot = slot_ref[e]
            rows = got_ref[pl.ds(slot, FIELDS, stride=CAP), :]
            high, low = halves(rows)
            both = lax.dot_general(
                jnp.concatenate([high, low], axis=0),
                w_ref[e],
                (((1,), (1,)), ((), ())),
                preferred_element_type=F32,
            )
            results.append((tile_ref[e], both[:FIELDS] + both[FIELDS:]))
        for tile, value in results:
            out_ref[tile] = out_ref[tile] + value
        return 0

    lax.fori_loop(0, entries // SUB, group, 0)


def regrid_back(got, weights, slots, tile_ids, tiles):
    return pl.pallas_call(
        regrid_kernel,
        out_shape=jax.ShapeDtypeStruct((tiles, FIELDS, LANES), F32),
        in_specs=[spec_vmem(), spec_vmem(), spec_smem(), spec_smem()],
        out_specs=spec_vmem(),
        compiler_params=params(16),
        name="regrid_back",
    )(got, weights, slots, tile_ids)


def exchange(x):
    return lax.all_to_all(x, BOTH, split_axis=0, concat_axis=0, tiled=True)


def per_device(
    atm_state,
    diffusivity,
    surface_prev,
    flux_mix,
    entry_dest,
    entry_tile,
    entry_row,
    regrid_blocks,
    ocean_state,
    land_mask,
    flux_response,
):
    devices = lax.axis_size("sec") * lax.axis_size("tile")
    _, levels, columns = atm_state.shape
    blocks, tiles = levels // SUB, columns // LANES
    _, depth, rows, _ = ocean_state.shape

    a_tiles = atm_state.reshape(FIELDS, blocks, SUB, tiles, LANES).transpose(0, 1, 3, 2, 4)
    d_tiles = diffusivity.reshape(blocks, SUB, tiles, LANES).transpose(0, 2, 1, 3)
    s_rows = surface_prev.reshape(FIELDS, tiles, LANES).transpose(1, 0, 2)
    s_rows = s_rows.reshape(tiles * FIELDS, LANES)
    y, e, outgoing, slots = atm_forward(
        a_tiles,
        d_tiles,
        s_rows,
        flux_mix,
        entry_dest[:, 0],
        entry_tile,
        entry_row,
        regrid_blocks,
        devices,
    )

    q = ocean_state.reshape(FIELDS * depth, rows, LANES)
    outgoing, q = lax.optimization_barrier((outgoing, q))
    chunk_rows = outgoing.shape[0] // devices
    incoming = exchange(outgoing.reshape(devices, chunk_rows // 2, 2, LANES))
    incoming = incoming.reshape(outgoing.shape)

    low_row, high_row, low_col, high_col = ocean_edges(q, land_mask)
    edges = (
        lax.ppermute(low_row, "sec", shift("sec", -1)),
        lax.ppermute(high_row, "sec", shift("sec", 1)),
        lax.ppermute(low_col, "tile", shift("tile", -1)),
        lax.ppermute(high_col, "tile", shift("tile", 1)),
    )
    bulk = ocean_bulk(q, flux_response)
    surf = ocean_top(q, land_mask, edges)
    atm_next = atm_back(y, e).transpose(0, 1, 3, 2, 4).reshape(FIELDS, levels, columns)

    top, returning = ocean_combine(incoming, bulk, surf, land_mask, flux_response, devices)
    arrived = exchange(returning)
    q_next = ocean_deep(q, land_mask, edges, top)
    back = regrid_back(
        arrived.reshape(devices * FIELDS * CAP, LANES), regrid_blocks, slots, entry_tile, tiles
    )
    surface_next = back.transpose(1, 0, 2).reshape(FIELDS, columns)
    return atm_next, q_next.reshape(ocean_state.shape), surface_next


def solution(mesh):
    return jax.shard_map(
        per_device,
        mesh=mesh,
        in_specs=(
            P(None, None, BOTH),
            P(None, BOTH),
            P(None, BOTH),
            P(),
            P(BOTH, None),
            P(BOTH),
            P(BOTH),
            P(BOTH, None, None),
            P(None, None, "sec", "tile"),
            P("sec", "tile"),
            P(),
        ),
        out_specs=(
            P(None, None, BOTH),
            P(None, None, "sec", "tile"),
            P(None, BOTH),
        ),
        check_vma=False,
    )
```

```python
import functools

import jax
import jax.numpy as jnp
from jax import lax
from jax.experimental import pallas as pl
from jax.experimental.pallas import tpu as pltpu
from jax.sharding import PartitionSpec as P

CAP = 4
LANES = 128
SUB = 8
FLUXES = 10
FEATURES = 12
FIELDS = 4
DIFFUSE = 0.2
CORIOLIS = 0.3
OCEAN_DT = 0.2
F32 = jnp.float32
BF16 = jnp.bfloat16
BOTH = ("sec", "tile")


def halves(x):
    high = x.astype(BF16)
    return high, (x - high.astype(F32)).astype(BF16)


def dot32(a, b):
    return jnp.dot(a, b, preferred_element_type=F32)


def spec_any():
    return pl.BlockSpec(memory_space=pltpu.HBM)


def spec_vmem():
    return pl.BlockSpec(memory_space=pltpu.VMEM)


def spec_smem():
    return pl.BlockSpec(memory_space=pltpu.SMEM)


def params(mib):
    return pltpu.CompilerParams(vmem_limit_bytes=mib * 2**20)


def eliminate(a_rows, d_rows, surface, tiles, blocks, first, groups, keep):
    def block(step, carry):
        lb = blocks - 1 - step
        bottom = jnp.where(lb == 0, 1.0, 0.0).astype(F32)
        carry = list(carry)
        for r in range(SUB - 1, -1, -1):
            for g in range(groups):
                tile = first + g * SUB
                grow, above, ys = carry[g]
                coup = d_rows[pl.ds((lb * tiles + tile) * SUB + r, SUB, stride=SUB), :]
                weight = 1.0 + above * grow
                inverse = 1.0 / (weight + coup)
                solved = []
                for v in range(FIELDS):
                    row = ((v * blocks + lb) * tiles + tile) * SUB + r
                    rhs = a_rows[pl.ds(row, SUB, stride=SUB), :]
                    if r == 0:
                        rhs = rhs + coup * (surface(v, tile) * bottom)
                    solved.append((rhs + above * ys[v]) * inverse)
                keep(lb, r, tile, coup * inverse, solved)
                carry[g] = (weight * inverse, coup, tuple(solved))
        return tuple(carry)

    zero = jnp.zeros((SUB, LANES), F32)
    start = tuple((zero, zero, (zero,) * FIELDS) for _ in range(groups))
    final = lax.fori_loop(0, blocks, block, start)
    return [(coup, x0) for _, coup, x0 in final]


def atm_kernel(
    chunks,
    chunk_rows,
    a_ref,
    d_ref,
    s_ref,
    mix_hbm,
    dest_hbm,
    tile_hbm,
    row_hbm,
    w_ref,
    out_hbm,
    a_buf,
    d_buf,
    s_buf,
    w_buf,
    y_buf,
    e_buf,
    flux,
    out_ref,
    mix_ref,
    dest_ref,
    tile_ref,
    row_ref,
    count,
    in_sems,
    sems,
):
    blocks, tiles = a_buf.shape[1], a_buf.shape[2]
    entries = w_buf.shape[0]
    per = tiles // chunks
    groups = per // SUB
    devices = count.shape[0]
    table_rows = chunk_rows - FLUXES * CAP
    me = lax.axis_index("sec") * lax.axis_size("tile") + lax.axis_index("tile")

    def surface(v, tile):
        return s_buf[pl.ds(tile * FIELDS + v, SUB, stride=FIELDS), :]

    def loads(ci):
        at = pl.ds(ci * per, per)
        return (
            pltpu.make_async_copy(d_ref.at[:, at], d_buf.at[:, at], in_sems.at[ci, 0]),
            pltpu.make_async_copy(a_ref.at[:, :, at], a_buf.at[:, :, at], in_sems.at[ci, 1]),
        )

    small = [
        pltpu.make_async_copy(src, dst, sems.at[i])
        for i, (src, dst) in enumerate(
            (
                (s_ref, s_buf),
                (mix_hbm, mix_ref),
                (dest_hbm, dest_ref),
                (tile_hbm, tile_ref),
                (row_hbm, row_ref),
            )
        )
    ]
    w_copy = pltpu.make_async_copy(w_ref, w_buf, sems.at[5])
    for copy in loads(0):
        copy.start()
    for copy in small:
        copy.start()
    for ci in range(1, chunks):
        for copy in loads(ci):
            copy.start()
    w_copy.start()

    a_rows = a_buf.reshape(FIELDS * blocks * tiles * SUB, LANES)
    d_rows = d_buf.reshape(blocks * tiles * SUB, LANES)
    for d in range(devices):
        count[d] = 0
    out_ref[...] = jnp.zeros_like(out_ref)
    for copy in small:
        copy.wait()

    def keep(lb, r, tile, coef, solved):
        if r == 1:
            e_buf[pl.ds(tile, SUB), :] = coef
            for v in range(FIELDS):
                y_buf[v, pl.ds(tile, SUB), :] = solved[v]

    def chunk(ci, _):
        for copy in loads(ci):
            copy.wait()
        first = ci * per
        final = eliminate(a_rows, d_rows, surface, tiles, blocks, first, groups, keep)
        for g in range(groups):
            tile = first + g * SUB
            coup, x0 = final[g]
            e1 = e_buf[pl.ds(tile, SUB), :]
            turb = [coup * (surface(v, tile) - x0[v]) for v in range(FIELDS)]
            x1 = [y_buf[v, pl.ds(tile, SUB), :] + e1 * x0[v] for v in range(FIELDS)]
            feats = turb + list(x0) + [turb[v] * x1[v] for v in range(FIELDS)]
            for f in range(FLUXES):
                total = mix_ref[f, 0] * feats[0]
                for k in range(1, FEATURES):
                    total = total + mix_ref[f, k] * feats[k]
                flux[pl.ds(tile * 16 + f, SUB, stride=16), :] = total
        return 0

    lax.fori_loop(0, chunks, chunk, 0)
    w_copy.wait()

    spot = lax.broadcasted_iota(jnp.int32, (table_rows, LANES), 0) * LANES
    spot = spot + lax.broadcasted_iota(jnp.int32, (table_rows, LANES), 1)

    def entry(e, _):
        d = dest_ref[e]
        k = count[d]
        count[d] = k + 1
        here = me * (2 * CAP) + k
        hit = (spot == here) | (spot == here + CAP)
        table = pl.ds(d * chunk_rows + FLUXES * CAP, table_rows)
        out_ref[table, :] += jnp.where(hit, row_ref[e] + 1, 0).astype(F32)
        picked = flux[pl.ds(pl.multiple_of(tile_ref[e] * 16, 16), 16), :]
        high, low = halves(picked)
        both = dot32(jnp.concatenate([high, low], axis=0), w_buf[e])
        both = both[:16] + both[16:]
        row = d * chunk_rows + k
        out_ref[pl.ds(row, SUB, stride=CAP), :] = both[:SUB]
        out_ref[pl.ds(row + SUB * CAP, FLUXES - SUB, stride=CAP), :] = both[SUB:FLUXES]
        return 0

    lax.fori_loop(0, entries, entry, 0, unroll=min(entries, 64))
    out_copy = pltpu.make_async_copy(out_ref, out_hbm, sems.at[6])
    out_copy.start()
    out_copy.wait()


def atm_forward(a_tiles, d_tiles, s_rows, mix, dest, tile_ids, row_ids, weights, devices):
    _, _, tiles, _, _ = a_tiles.shape
    entries = weights.shape[0]
    chunks = 4
    chunk_rows = FLUXES * CAP + devices * 2 * CAP // LANES
    out_shape = (devices * chunk_rows, LANES)
    return pl.pallas_call(
        functools.partial(atm_kernel, chunks, chunk_rows),
        out_shape=jax.ShapeDtypeStruct(out_shape, F32),
        in_specs=[spec_any()] * 8,
        out_specs=spec_any(),
        scratch_shapes=[
            pltpu.VMEM(a_tiles.shape, F32),
            pltpu.VMEM(d_tiles.shape, F32),
            pltpu.VMEM(s_rows.shape, F32),
            pltpu.VMEM(weights.shape, BF16),
            pltpu.VMEM((FIELDS, tiles, LANES), F32),
            pltpu.VMEM((tiles, LANES), F32),
            pltpu.VMEM((tiles * 16, LANES), F32),
            pltpu.VMEM(out_shape, F32),
            pltpu.SMEM(mix.shape, F32),
            pltpu.SMEM((entries,), jnp.int32),
            pltpu.SMEM((entries,), jnp.int32),
            pltpu.SMEM((entries,), jnp.int32),
            pltpu.SMEM((devices,), jnp.int32),
            pltpu.SemaphoreType.DMA((chunks, 2)),
            pltpu.SemaphoreType.DMA((7,)),
        ],
        compiler_params=params(60),
        name="atm_forward",
    )(a_tiles, d_tiles, s_rows, mix, dest, tile_ids, row_ids, weights)


def solve_kernel(a_ref, d_ref, s_ref, out_ref, y_buf, e_buf):
    blocks, tiles = out_ref.shape[1], out_ref.shape[2]
    a_rows = a_ref.reshape(FIELDS * blocks * tiles * SUB, LANES)
    d_rows = d_ref.reshape(blocks * tiles * SUB, LANES)
    rows = out_ref.reshape(FIELDS * blocks * tiles * SUB, LANES)
    groups = tiles // SUB

    def surface(v, tile):
        return s_ref[pl.ds(tile * FIELDS + v, SUB, stride=FIELDS), :]

    def keep(lb, r, tile, coef, solved):
        level = lb * SUB + r
        e_buf[level, pl.ds(tile, SUB), :] = coef
        for v in range(FIELDS):
            y_buf[v, level, pl.ds(tile, SUB), :] = solved[v]

    eliminate(a_rows, d_rows, surface, tiles, blocks, 0, groups, keep)

    def block(lb, carry):
        carry = list(carry)
        for r in range(SUB):
            for g in range(groups):
                coef = e_buf[lb * SUB + r, pl.ds(g * SUB, SUB), :]
                if r == 0:
                    coef = coef * jnp.where(lb == 0, 0.0, 1.0).astype(F32)
                for v in range(FIELDS):
                    x = y_buf[v, lb * SUB + r, pl.ds(g * SUB, SUB), :]
                    x = x + coef * carry[g * FIELDS + v]
                    row = ((v * blocks + lb) * tiles + g * SUB) * SUB + r
                    rows[pl.ds(row, SUB, stride=SUB), :] = x
                    carry[g * FIELDS + v] = x
        return tuple(carry)

    zero = jnp.zeros((SUB, LANES), F32)
    lax.fori_loop(0, blocks, block, (zero,) * (groups * FIELDS))


def atm_solve(a_tiles, d_tiles, s_rows):
    _, blocks, tiles, _, _ = a_tiles.shape
    levels = blocks * SUB
    per = 16
    return pl.pallas_call(
        solve_kernel,
        grid=(tiles // per,),
        out_shape=jax.ShapeDtypeStruct(a_tiles.shape, F32),
        in_specs=[
            pl.BlockSpec((FIELDS, blocks, per, SUB, LANES), lambda i: (0, 0, i, 0, 0)),
            pl.BlockSpec((blocks, per, SUB, LANES), lambda i: (0, i, 0, 0)),
            pl.BlockSpec((per * FIELDS, LANES), lambda i: (i, 0)),
        ],
        out_specs=pl.BlockSpec((FIELDS, blocks, per, SUB, LANES), lambda i: (0, 0, i, 0, 0)),
        scratch_shapes=[
            pltpu.VMEM((FIELDS, levels, per, LANES), F32),
            pltpu.VMEM((levels, per, LANES), F32),
        ],
        compiler_params=params(60),
        cost_estimate=pl.CostEstimate(
            flops=8 * a_tiles.size, bytes_accessed=9 * a_tiles.size, transcendentals=0
        ),
        name="atm_solve",
    )(a_tiles, d_tiles, s_rows)


def edge_kernel(q_ref, m_ref, low_row, high_row, low_col, high_col):
    fields, rows, _ = q_ref.shape
    mask = m_ref[...].astype(F32)
    for dst, at in ((low_row, 0), (high_row, rows - 1)):
        dst[...] = jnp.zeros_like(dst)
        for i in range(fields):
            dst[i : i + 1, :] = q_ref[i, at : at + 1, :]
        dst[fields : fields + 1, :] = mask[at : at + 1, :]

    lane = lax.broadcasted_iota(jnp.int32, (rows, LANES), 1)
    low = jnp.zeros((rows, LANES), F32)
    high = jnp.zeros((rows, LANES), F32)
    for i in range(fields + 1):
        cells = q_ref[i] if i < fields else mask
        turned = pltpu.roll(cells, i, 1) if i else cells
        low = jnp.where(lane == i, turned, low)
        high = jnp.where(lane == (i + LANES - 1) % LANES, turned, high)
    low_col[...] = low
    high_col[...] = high


def ocean_edges(q, mask):
    pad = -(-(q.shape[0] + 1) // SUB) * SUB
    row = jax.ShapeDtypeStruct((pad, LANES), F32)
    col = jax.ShapeDtypeStruct(mask.shape, F32)
    return pl.pallas_call(
        edge_kernel,
        out_shape=(row, row, col, col),
        in_specs=[spec_vmem(), spec_vmem()],
        out_specs=(spec_vmem(),) * 4,
        compiler_params=params(8),
        cost_estimate=pl.CostEstimate(flops=q.size, bytes_accessed=4 * q.size, transcendentals=0),
        name="ocean_edges",
    )(q, mask)


def shift(axis, step):
    count = lax.axis_size(axis)
    if step > 0:
        return [(i, i + 1) for i in range(count - 1)]
    return [(i + 1, i) for i in range(count - 1)]


def bulk_kernel(q_ref, resp_ref, dest_ref, bulk_ref, rows_ref, slot_ref, count):
    depth = q_ref.shape[0] // FIELDS
    for g in range(FIELDS):
        for f in range(FLUXES):
            i = g * FLUXES + f
            rows_ref[i : i + 1, :] = jnp.full((1, LANES), resp_ref[g, f], F32)
    tops = [q_ref[v * depth] for v in range(FIELDS)]
    for f in range(FLUXES):
        total = resp_ref[0, f] * tops[0]
        for v in range(1, FIELDS):
            total = total + resp_ref[v, f] * tops[v]
        bulk_ref[f] = 1.0 + 0.5 * jnp.tanh(total)

    for d in range(count.shape[0]):
        count[d] = 0

    def entry(e, _):
        d = dest_ref[e]
        k = count[d]
        count[d] = k + 1
        slot_ref[e] = d * (FIELDS * CAP) + k
        return 0

    lax.fori_loop(0, dest_ref.shape[0], entry, 0)


def ocean_bulk(q, response, dest, devices):
    return pl.pallas_call(
        bulk_kernel,
        out_shape=(
            jax.ShapeDtypeStruct((FLUXES,) + q.shape[1:], F32),
            jax.ShapeDtypeStruct((FIELDS * FLUXES, LANES), F32),
            jax.ShapeDtypeStruct(dest.shape, jnp.int32),
        ),
        in_specs=[spec_vmem(), spec_smem(), spec_smem()],
        out_specs=(spec_vmem(), spec_vmem(), spec_smem()),
        scratch_shapes=[pltpu.SMEM((devices,), jnp.int32)],
        compiler_params=params(8),
        cost_estimate=pl.CostEstimate(
            flops=3 * q.size, bytes_accessed=2 * q.size, transcendentals=q.size // 3
        ),
        name="ocean_bulk",
    )(q, response, dest)


def stencil(levels, q_ref, m_ref, east_ref, west_ref, north_ref, south_ref, save):
    fields, rows, _ = q_ref.shape
    depth = fields // FIELDS
    lane = lax.broadcasted_iota(jnp.int32, (rows, LANES), 1)
    last, first = lane == LANES - 1, lane == 0

    def around(cells, i):
        high = (i + LANES - 1) % LANES
        east = jnp.concatenate([cells[1:], east_ref[i : i + 1, :]], axis=0)
        west = jnp.concatenate([west_ref[i : i + 1, :], cells[:-1]], axis=0)
        north = jnp.where(last, north_ref[:, i : i + 1], pltpu.roll(cells, LANES - 1, 1))
        south = jnp.where(first, south_ref[:, high : high + 1], pltpu.roll(cells, 1, 1))
        return east, west, north, south

    mask = m_ref[...].astype(F32)
    m_east, m_west, m_north, m_south = around(mask, fields)
    m_all = m_east + m_west + m_north + m_south
    for level in levels:
        zonal = q_ref[2 * depth + level]
        merid = q_ref[3 * depth + level]
        for v in range(FIELDS):
            i = v * depth + level
            cells = q_ref[i]
            east, west, north, south = around(cells, i)
            lap = m_east * east + m_west * west + m_north * north + m_south * south
            lap = lap - m_all * cells
            adv = 0.5 * (zonal * (east - west) + merid * (north - south))
            tend = DIFFUSE * lap - adv
            if v == 2:
                tend = tend + CORIOLIS * merid
            if v == 3:
                tend = tend - CORIOLIS * zonal
            save(v, level, mask * (cells + OCEAN_DT * tend))


def top_kernel(q_ref, m_ref, east_ref, west_ref, north_ref, south_ref, surf_ref):
    def save(v, level, value):
        surf_ref[v] = value

    stencil((0,), q_ref, m_ref, east_ref, west_ref, north_ref, south_ref, save)


def ocean_top(q, mask, edges):
    return pl.pallas_call(
        top_kernel,
        out_shape=jax.ShapeDtypeStruct((FIELDS,) + q.shape[1:], F32),
        in_specs=[spec_vmem()] * 6,
        out_specs=spec_vmem(),
        compiler_params=params(8),
        cost_estimate=pl.CostEstimate(flops=4 * q.size, bytes_accessed=q.size, transcendentals=0),
        name="ocean_top",
    )(q, mask, *edges)


def deep_kernel(q_ref, m_ref, east_ref, west_ref, north_ref, south_ref, top_ref, out_ref):
    depth = q_ref.shape[0] // FIELDS

    def save(v, level, value):
        out_ref[v * depth + level] = value

    for v in range(FIELDS):
        out_ref[v * depth] = top_ref[v]
    levels = range(1, depth)
    stencil(levels, q_ref, m_ref, east_ref, west_ref, north_ref, south_ref, save)


def ocean_deep(q, mask, edges, top):
    return pl.pallas_call(
        deep_kernel,
        out_shape=jax.ShapeDtypeStruct(q.shape, F32),
        in_specs=[spec_vmem()] * 7,
        out_specs=spec_vmem(),
        compiler_params=params(8),
        cost_estimate=pl.CostEstimate(
            flops=30 * q.size, bytes_accessed=8 * q.size, transcendentals=0
        ),
        name="ocean_deep",
    )(q, mask, *edges, top)


def combine_kernel(
    got_ref, bulk_ref, surf_ref, m_ref, resp_ref, top, back_ref
):
    rows = m_ref.shape[0]
    sources = back_ref.shape[0]
    chunk_rows = got_ref.shape[0] // sources
    table_rows = chunk_rows - FLUXES * CAP

    x = lax.broadcasted_iota(jnp.int32, (2 * rows, LANES), 0)
    spot = lax.broadcasted_iota(jnp.int32, (2 * rows, LANES), 1)
    pair = (spot // CAP) % 2 == x // rows
    wanted = jnp.where(pair, (x % rows + 1).astype(F32), -1.0)
    hots = []
    for j in range(table_rows):
        seen = got_ref[pl.ds(FLUXES * CAP + j, sources, stride=chunk_rows), :]
        seen = jnp.sum(seen, axis=0, keepdims=True)
        hots.append((seen == wanted).astype(F32))
    hot = jnp.concatenate([h.astype(BF16) for h in hots], axis=1)

    force = [None] * FIELDS
    for j in range(FLUXES // 2):
        data = jnp.concatenate(
            [got_ref[pl.ds(s * chunk_rows + j * SUB, SUB), :] for s in range(sources)], axis=0
        )
        high, low = halves(data)
        both = dot32(hot, high) + dot32(hot, low)
        for p in range(2):
            f = 2 * j + p
            drive = both[p * rows : (p + 1) * rows] * bulk_ref[f]
            for g in range(FIELDS):
                term = resp_ref[g * FLUXES + f, :][None, :] * drive
                force[g] = term if f == 0 else force[g] + term
    mask = m_ref[...].astype(F32)
    for g in range(FIELDS):
        top[g] = surf_ref[g] + mask * force[g]
    hot_t = jnp.concatenate([jnp.transpose(h).astype(BF16) for h in hots], axis=0)
    for j in range(FIELDS // 2):
        pair = jnp.concatenate([top[2 * j], top[2 * j + 1]], axis=0)
        high, low = halves(pair)
        both = dot32(hot_t, high) + dot32(hot_t, low)
        back_ref[:, j * SUB : (j + 1) * SUB, :] = both.reshape(sources, SUB, LANES)


def ocean_combine(got, bulk, surf, mask, response, sources):
    return pl.pallas_call(
        combine_kernel,
        out_shape=(
            jax.ShapeDtypeStruct(surf.shape, F32),
            jax.ShapeDtypeStruct((sources, FIELDS * CAP, LANES), F32),
        ),
        in_specs=[spec_vmem()] * 5,
        out_specs=(spec_vmem(), spec_vmem()),
        compiler_params=params(16),
        cost_estimate=pl.CostEstimate(
            flops=4 * got.size, bytes_accessed=4 * got.size, transcendentals=0
        ),
        name="ocean_combine",
    )(got, bulk, surf, mask, response)


def regrid_kernel(got_ref, w_ref, slot_hbm, tile_hbm, out_ref, slot_ref, tile_ref, sems):
    entries = w_ref.shape[0]
    copies = (
        pltpu.make_async_copy(slot_hbm, slot_ref, sems.at[0]),
        pltpu.make_async_copy(tile_hbm, tile_ref, sems.at[1]),
    )
    for copy in copies:
        copy.start()
    out_ref[...] = jnp.zeros_like(out_ref)
    for copy in copies:
        copy.wait()

    def group(i, _):
        results = []
        for u in range(SUB):
            e = i * SUB + u
            slot = slot_ref[e]
            rows = got_ref[pl.ds(slot, FIELDS, stride=CAP), :]
            high, low = halves(rows)
            both = lax.dot_general(
                jnp.concatenate([high, low], axis=0),
                w_ref[e],
                (((1,), (1,)), ((), ())),
                preferred_element_type=F32,
            )
            results.append((tile_ref[e], both[:FIELDS] + both[FIELDS:]))
        for tile, value in results:
            out_ref[tile] = out_ref[tile] + value
        return 0

    lax.fori_loop(0, entries // SUB, group, 0, unroll=min(entries // SUB, 8))


def regrid_back(got, weights, slots, tile_ids, tiles):
    return pl.pallas_call(
        regrid_kernel,
        out_shape=jax.ShapeDtypeStruct((tiles, FIELDS, LANES), F32),
        in_specs=[spec_vmem(), spec_vmem(), spec_any(), spec_any()],
        out_specs=spec_vmem(),
        scratch_shapes=[
            pltpu.SMEM(slots.shape, jnp.int32),
            pltpu.SMEM(slots.shape, jnp.int32),
            pltpu.SemaphoreType.DMA((2,)),
        ],
        compiler_params=params(16),
        name="regrid_back",
    )(got, weights, slots, tile_ids)


def exchange(x):
    return lax.all_to_all(x, BOTH, split_axis=0, concat_axis=0, tiled=True)


def per_device(
    atm_state,
    diffusivity,
    surface_prev,
    flux_mix,
    entry_dest,
    entry_tile,
    entry_row,
    regrid_blocks,
    ocean_state,
    land_mask,
    flux_response,
):
    devices = lax.axis_size("sec") * lax.axis_size("tile")
    _, levels, columns = atm_state.shape
    blocks, tiles = levels // SUB, columns // LANES
    _, depth, rows, _ = ocean_state.shape

    a_tiles = atm_state.reshape(FIELDS, blocks, SUB, tiles, LANES).transpose(0, 1, 3, 2, 4)
    d_tiles = diffusivity.reshape(blocks, SUB, tiles, LANES).transpose(0, 2, 1, 3)
    s_rows = surface_prev.reshape(FIELDS, tiles, LANES).transpose(1, 0, 2)
    s_rows = s_rows.reshape(tiles * FIELDS, LANES)
    dest = entry_dest[:, 0]
    outgoing = atm_forward(
        a_tiles, d_tiles, s_rows, flux_mix, dest, entry_tile, entry_row, regrid_blocks, devices
    )

    q = ocean_state.reshape(FIELDS * depth, rows, LANES)
    outgoing, q = lax.optimization_barrier((outgoing, q))
    chunk_rows = outgoing.shape[0] // devices
    incoming = exchange(outgoing.reshape(devices, chunk_rows // 2, 2, LANES))
    incoming = incoming.reshape(outgoing.shape)

    low_row, high_row, low_col, high_col = ocean_edges(q, land_mask)
    edges = (
        lax.ppermute(low_row, "sec", shift("sec", -1)),
        lax.ppermute(high_row, "sec", shift("sec", 1)),
        lax.ppermute(low_col, "tile", shift("tile", -1)),
        lax.ppermute(high_col, "tile", shift("tile", 1)),
    )
    bulk, resp_rows, slots = ocean_bulk(q, flux_response, dest, devices)
    surf = ocean_top(q, land_mask, edges)
    top, returning = ocean_combine(incoming, bulk, surf, land_mask, resp_rows, devices)
    arrived = exchange(returning)
    q_next = ocean_deep(q, land_mask, edges, top)
    q_next, a_tiles, d_tiles, s_rows = lax.optimization_barrier(
        (q_next, a_tiles, d_tiles, s_rows)
    )
    atm_next = atm_solve(a_tiles, d_tiles, s_rows).transpose(0, 1, 3, 2, 4).reshape(FIELDS, levels, columns)
    back = regrid_back(
        arrived.reshape(devices * FIELDS * CAP, LANES), regrid_blocks, slots, entry_tile, tiles
    )
    surface_next = back.transpose(1, 0, 2).reshape(FIELDS, columns)
    return atm_next, q_next.reshape(ocean_state.shape), surface_next


def solution(mesh):
    return jax.shard_map(
        per_device,
        mesh=mesh,
        in_specs=(
            P(None, None, BOTH),
            P(None, BOTH),
            P(None, BOTH),
            P(),
            P(BOTH, None),
            P(BOTH),
            P(BOTH),
            P(BOTH, None, None),
            P(None, None, "sec", "tile"),
            P("sec", "tile"),
            P(),
        ),
        out_specs=(
            P(None, None, BOTH),
            P(None, None, "sec", "tile"),
            P(None, BOTH),
        ),
        check_vma=False,
    )
```

```python
import functools

import jax
import jax.numpy as jnp
from jax import lax
from jax.experimental import pallas as pl
from jax.experimental.pallas import tpu as pltpu
from jax.sharding import PartitionSpec as P

CAP = 4
LANES = 128
SUB = 8
FLUXES = 10
FEATURES = 12
FIELDS = 4
DIFFUSE = 0.2
CORIOLIS = 0.3
OCEAN_DT = 0.2
F32 = jnp.float32
BF16 = jnp.bfloat16
BOTH = ("sec", "tile")


def halves(x):
    high = x.astype(BF16)
    return high, (x - high.astype(F32)).astype(BF16)


def dot32(a, b):
    return jnp.dot(a, b, preferred_element_type=F32)


def spec_any():
    return pl.BlockSpec(memory_space=pltpu.HBM)


def spec_vmem():
    return pl.BlockSpec(memory_space=pltpu.VMEM)


def spec_smem():
    return pl.BlockSpec(memory_space=pltpu.SMEM)


def params(mib):
    return pltpu.CompilerParams(vmem_limit_bytes=mib * 2**20)


def eliminate(a_rows, d_rows, surface, tiles, blocks, first, groups, keep):
    def block(step, carry):
        lb = blocks - 1 - step
        bottom = jnp.where(lb == 0, 1.0, 0.0).astype(F32)
        carry = list(carry)
        for r in range(SUB - 1, -1, -1):
            for g in range(groups):
                tile = first + g * SUB
                grow, above, ys = carry[g]
                coup = d_rows[pl.ds((lb * tiles + tile) * SUB + r, SUB, stride=SUB), :]
                weight = 1.0 + above * grow
                inverse = 1.0 / (weight + coup)
                solved = []
                for v in range(FIELDS):
                    row = ((v * blocks + lb) * tiles + tile) * SUB + r
                    rhs = a_rows[pl.ds(row, SUB, stride=SUB), :]
                    if r == 0:
                        rhs = rhs + coup * (surface(v, tile) * bottom)
                    solved.append((rhs + above * ys[v]) * inverse)
                keep(lb, r, tile, coup * inverse, solved)
                carry[g] = (weight * inverse, coup, tuple(solved))
        return tuple(carry)

    zero = jnp.zeros((SUB, LANES), F32)
    start = tuple((zero, zero, (zero,) * FIELDS) for _ in range(groups))
    final = lax.fori_loop(0, blocks, block, start)
    return [(coup, x0) for _, coup, x0 in final]


def atm_kernel(
    chunks,
    chunk_rows,
    a_ref,
    d_ref,
    s_ref,
    mix_hbm,
    dest_hbm,
    tile_hbm,
    row_hbm,
    w_ref,
    out_hbm,
    a_buf,
    d_buf,
    s_buf,
    w_buf,
    y_buf,
    e_buf,
    flux,
    out_ref,
    mix_ref,
    dest_ref,
    tile_ref,
    row_ref,
    count,
    in_sems,
    sems,
):
    blocks, tiles = a_buf.shape[1], a_buf.shape[2]
    entries = w_buf.shape[0]
    per = tiles // chunks
    groups = per // SUB
    devices = count.shape[0]
    table_rows = chunk_rows - FLUXES * CAP
    me = lax.axis_index("sec") * lax.axis_size("tile") + lax.axis_index("tile")

    def surface(v, tile):
        return s_buf[pl.ds(tile * FIELDS + v, SUB, stride=FIELDS), :]

    def loads(ci):
        at = pl.ds(ci * per, per)
        return (
            pltpu.make_async_copy(d_ref.at[:, at], d_buf.at[:, at], in_sems.at[ci, 0]),
            pltpu.make_async_copy(a_ref.at[:, :, at], a_buf.at[:, :, at], in_sems.at[ci, 1]),
        )

    small = [
        pltpu.make_async_copy(src, dst, sems.at[i])
        for i, (src, dst) in enumerate(
            (
                (s_ref, s_buf),
                (mix_hbm, mix_ref),
                (dest_hbm, dest_ref),
                (tile_hbm, tile_ref),
                (row_hbm, row_ref),
            )
        )
    ]
    w_copy = pltpu.make_async_copy(w_ref, w_buf, sems.at[5])
    for copy in loads(0):
        copy.start()
    for copy in small:
        copy.start()
    for ci in range(1, chunks):
        for copy in loads(ci):
            copy.start()
    w_copy.start()

    a_rows = a_buf.reshape(FIELDS * blocks * tiles * SUB, LANES)
    d_rows = d_buf.reshape(blocks * tiles * SUB, LANES)
    for d in range(devices):
        count[d] = 0
    out_ref[...] = jnp.zeros_like(out_ref)
    for copy in small:
        copy.wait()

    def keep(lb, r, tile, coef, solved):
        if r == 1:
            e_buf[pl.ds(tile, SUB), :] = coef
            for v in range(FIELDS):
                y_buf[v, pl.ds(tile, SUB), :] = solved[v]

    def chunk(ci, _):
        for copy in loads(ci):
            copy.wait()
        first = ci * per
        final = eliminate(a_rows, d_rows, surface, tiles, blocks, first, groups, keep)
        for g in range(groups):
            tile = first + g * SUB
            coup, x0 = final[g]
            e1 = e_buf[pl.ds(tile, SUB), :]
            turb = [coup * (surface(v, tile) - x0[v]) for v in range(FIELDS)]
            x1 = [y_buf[v, pl.ds(tile, SUB), :] + e1 * x0[v] for v in range(FIELDS)]
            feats = turb + list(x0) + [turb[v] * x1[v] for v in range(FIELDS)]
            for f in range(FLUXES):
                total = mix_ref[f, 0] * feats[0]
                for k in range(1, FEATURES):
                    total = total + mix_ref[f, k] * feats[k]
                flux[pl.ds(tile * 16 + f, SUB, stride=16), :] = total
        return 0

    lax.fori_loop(0, chunks, chunk, 0)
    w_copy.wait()

    spot = lax.broadcasted_iota(jnp.int32, (table_rows, LANES), 0) * LANES
    spot = spot + lax.broadcasted_iota(jnp.int32, (table_rows, LANES), 1)

    def entry(e, _):
        d = dest_ref[e]
        k = count[d]
        count[d] = k + 1
        here = me * (2 * CAP) + k
        hit = (spot == here) | (spot == here + CAP)
        table = pl.ds(d * chunk_rows + FLUXES * CAP, table_rows)
        out_ref[table, :] += jnp.where(hit, row_ref[e] + 1, 0).astype(F32)
        picked = flux[pl.ds(pl.multiple_of(tile_ref[e] * 16, 16), 16), :]
        high, low = halves(picked)
        both = dot32(jnp.concatenate([high, low], axis=0), w_buf[e])
        both = both[:16] + both[16:]
        row = d * chunk_rows + k
        out_ref[pl.ds(row, SUB, stride=CAP), :] = both[:SUB]
        out_ref[pl.ds(row + SUB * CAP, FLUXES - SUB, stride=CAP), :] = both[SUB:FLUXES]
        return 0

    lax.fori_loop(0, entries, entry, 0, unroll=min(entries, 64))
    out_copy = pltpu.make_async_copy(out_ref, out_hbm, sems.at[6])
    out_copy.start()
    out_copy.wait()


def atm_forward(a_tiles, d_tiles, s_rows, mix, dest, tile_ids, row_ids, weights, devices):
    _, _, tiles, _, _ = a_tiles.shape
    entries = weights.shape[0]
    chunks = 4
    chunk_rows = FLUXES * CAP + devices * 2 * CAP // LANES
    out_shape = (devices * chunk_rows, LANES)
    return pl.pallas_call(
        functools.partial(atm_kernel, chunks, chunk_rows),
        out_shape=jax.ShapeDtypeStruct(out_shape, F32),
        in_specs=[spec_any()] * 8,
        out_specs=spec_any(),
        scratch_shapes=[
            pltpu.VMEM(a_tiles.shape, F32),
            pltpu.VMEM(d_tiles.shape, F32),
            pltpu.VMEM(s_rows.shape, F32),
            pltpu.VMEM(weights.shape, BF16),
            pltpu.VMEM((FIELDS, tiles, LANES), F32),
            pltpu.VMEM((tiles, LANES), F32),
            pltpu.VMEM((tiles * 16, LANES), F32),
            pltpu.VMEM(out_shape, F32),
            pltpu.SMEM(mix.shape, F32),
            pltpu.SMEM((entries,), jnp.int32),
            pltpu.SMEM((entries,), jnp.int32),
            pltpu.SMEM((entries,), jnp.int32),
            pltpu.SMEM((devices,), jnp.int32),
            pltpu.SemaphoreType.DMA((chunks, 2)),
            pltpu.SemaphoreType.DMA((7,)),
        ],
        compiler_params=params(60),
        name="atm_forward",
    )(a_tiles, d_tiles, s_rows, mix, dest, tile_ids, row_ids, weights)


def solve_kernel(a_ref, d_ref, s_ref, out_ref, y_buf, e_buf):
    blocks, tiles = out_ref.shape[1], out_ref.shape[2]
    a_rows = a_ref.reshape(FIELDS * blocks * tiles * SUB, LANES)
    d_rows = d_ref.reshape(blocks * tiles * SUB, LANES)
    rows = out_ref.reshape(FIELDS * blocks * tiles * SUB, LANES)
    groups = tiles // SUB

    def surface(v, tile):
        return s_ref[pl.ds(tile * FIELDS + v, SUB, stride=FIELDS), :]

    def keep(lb, r, tile, coef, solved):
        level = lb * SUB + r
        e_buf[level, pl.ds(tile, SUB), :] = coef
        for v in range(FIELDS):
            y_buf[v, level, pl.ds(tile, SUB), :] = solved[v]

    eliminate(a_rows, d_rows, surface, tiles, blocks, 0, groups, keep)

    def block(lb, carry):
        carry = list(carry)
        for r in range(SUB):
            for g in range(groups):
                coef = e_buf[lb * SUB + r, pl.ds(g * SUB, SUB), :]
                if r == 0:
                    coef = coef * jnp.where(lb == 0, 0.0, 1.0).astype(F32)
                for v in range(FIELDS):
                    x = y_buf[v, lb * SUB + r, pl.ds(g * SUB, SUB), :]
                    x = x + coef * carry[g * FIELDS + v]
                    row = ((v * blocks + lb) * tiles + g * SUB) * SUB + r
                    rows[pl.ds(row, SUB, stride=SUB), :] = x
                    carry[g * FIELDS + v] = x
        return tuple(carry)

    zero = jnp.zeros((SUB, LANES), F32)
    lax.fori_loop(0, blocks, block, (zero,) * (groups * FIELDS))


def atm_solve(a_tiles, d_tiles, s_rows):
    _, blocks, tiles, _, _ = a_tiles.shape
    levels = blocks * SUB
    per = 16
    return pl.pallas_call(
        solve_kernel,
        grid=(tiles // per,),
        out_shape=jax.ShapeDtypeStruct(a_tiles.shape, F32),
        in_specs=[
            pl.BlockSpec((FIELDS, blocks, per, SUB, LANES), lambda i: (0, 0, i, 0, 0)),
            pl.BlockSpec((blocks, per, SUB, LANES), lambda i: (0, i, 0, 0)),
            pl.BlockSpec((per * FIELDS, LANES), lambda i: (i, 0)),
        ],
        out_specs=pl.BlockSpec((FIELDS, blocks, per, SUB, LANES), lambda i: (0, 0, i, 0, 0)),
        scratch_shapes=[
            pltpu.VMEM((FIELDS, levels, per, LANES), F32),
            pltpu.VMEM((levels, per, LANES), F32),
        ],
        compiler_params=params(60),
        cost_estimate=pl.CostEstimate(
            flops=8 * a_tiles.size, bytes_accessed=9 * a_tiles.size, transcendentals=0
        ),
        name="atm_solve",
    )(a_tiles, d_tiles, s_rows)


def edge_kernel(q_ref, m_ref, low_row, high_row, low_col, high_col):
    fields, rows, _ = q_ref.shape
    mask = m_ref[...].astype(F32)
    for dst, at in ((low_row, 0), (high_row, rows - 1)):
        dst[...] = jnp.zeros_like(dst)
        for i in range(fields):
            dst[i : i + 1, :] = q_ref[i, at : at + 1, :]
        dst[fields : fields + 1, :] = mask[at : at + 1, :]

    lane = lax.broadcasted_iota(jnp.int32, (rows, LANES), 1)
    low = jnp.zeros((rows, LANES), F32)
    high = jnp.zeros((rows, LANES), F32)
    for i in range(fields + 1):
        cells = q_ref[i] if i < fields else mask
        turned = pltpu.roll(cells, i, 1) if i else cells
        low = jnp.where(lane == i, turned, low)
        high = jnp.where(lane == (i + LANES - 1) % LANES, turned, high)
    low_col[...] = low
    high_col[...] = high


def ocean_edges(q, mask):
    pad = -(-(q.shape[0] + 1) // SUB) * SUB
    row = jax.ShapeDtypeStruct((pad, LANES), F32)
    col = jax.ShapeDtypeStruct(mask.shape, F32)
    return pl.pallas_call(
        edge_kernel,
        out_shape=(row, row, col, col),
        in_specs=[spec_vmem(), spec_vmem()],
        out_specs=(spec_vmem(),) * 4,
        compiler_params=params(8),
        cost_estimate=pl.CostEstimate(flops=q.size, bytes_accessed=4 * q.size, transcendentals=0),
        name="ocean_edges",
    )(q, mask)


def shift(axis, step):
    count = lax.axis_size(axis)
    if step > 0:
        return [(i, i + 1) for i in range(count - 1)]
    return [(i + 1, i) for i in range(count - 1)]


def bulk_kernel(q_ref, resp_ref, dest_ref, bulk_ref, rows_ref, pick_ref, wide, count):
    depth = q_ref.shape[0] // FIELDS
    for g in range(FIELDS):
        for f in range(FLUXES):
            i = g * FLUXES + f
            rows_ref[i : i + 1, :] = jnp.full((1, LANES), resp_ref[g, f], F32)
    tops = [q_ref[v * depth] for v in range(FIELDS)]
    for f in range(FLUXES):
        total = resp_ref[0, f] * tops[0]
        for v in range(1, FIELDS):
            total = total + resp_ref[v, f] * tops[v]
        bulk_ref[f] = 1.0 + 0.5 * jnp.tanh(total)

    entries = dest_ref.shape[0]
    lane = lax.broadcasted_iota(jnp.int32, (1, wide.shape[1]), 1)
    for d in range(count.shape[0]):
        count[d] = 0

    def entry(e, _):
        d = dest_ref[e]
        k = count[d]
        count[d] = k + 1
        for p in range(2):
            here = d * (2 * CAP) + p * CAP + k
            wide[pl.ds(p * entries + e, 1), :] = (lane == here).astype(F32)
        return 0

    lax.fori_loop(0, entries, entry, 0, unroll=4)
    pick_ref[...] = wide[...].astype(BF16)


def ocean_bulk(q, response, dest, devices):
    picks = (2 * dest.shape[0], devices * 2 * CAP)
    return pl.pallas_call(
        bulk_kernel,
        out_shape=(
            jax.ShapeDtypeStruct((FLUXES,) + q.shape[1:], F32),
            jax.ShapeDtypeStruct((FIELDS * FLUXES, LANES), F32),
            jax.ShapeDtypeStruct(picks, BF16),
        ),
        in_specs=[spec_vmem(), spec_smem(), spec_smem()],
        out_specs=(spec_vmem(),) * 3,
        scratch_shapes=[pltpu.VMEM(picks, F32), pltpu.SMEM((devices,), jnp.int32)],
        compiler_params=params(8),
        cost_estimate=pl.CostEstimate(
            flops=3 * q.size, bytes_accessed=2 * q.size, transcendentals=q.size // 3
        ),
        name="ocean_bulk",
    )(q, response, dest)


def stencil(levels, q_ref, m_ref, east_ref, west_ref, north_ref, south_ref, save):
    fields, rows, _ = q_ref.shape
    depth = fields // FIELDS
    lane = lax.broadcasted_iota(jnp.int32, (rows, LANES), 1)
    last, first = lane == LANES - 1, lane == 0

    def around(cells, i):
        high = (i + LANES - 1) % LANES
        east = jnp.concatenate([cells[1:], east_ref[i : i + 1, :]], axis=0)
        west = jnp.concatenate([west_ref[i : i + 1, :], cells[:-1]], axis=0)
        north = jnp.where(last, north_ref[:, i : i + 1], pltpu.roll(cells, LANES - 1, 1))
        south = jnp.where(first, south_ref[:, high : high + 1], pltpu.roll(cells, 1, 1))
        return east, west, north, south

    mask = m_ref[...].astype(F32)
    m_east, m_west, m_north, m_south = around(mask, fields)
    m_all = m_east + m_west + m_north + m_south
    for level in levels:
        zonal = q_ref[2 * depth + level]
        merid = q_ref[3 * depth + level]
        for v in range(FIELDS):
            i = v * depth + level
            cells = q_ref[i]
            east, west, north, south = around(cells, i)
            lap = m_east * east + m_west * west + m_north * north + m_south * south
            lap = lap - m_all * cells
            adv = 0.5 * (zonal * (east - west) + merid * (north - south))
            tend = DIFFUSE * lap - adv
            if v == 2:
                tend = tend + CORIOLIS * merid
            if v == 3:
                tend = tend - CORIOLIS * zonal
            save(v, level, mask * (cells + OCEAN_DT * tend))


def top_kernel(q_ref, m_ref, east_ref, west_ref, north_ref, south_ref, surf_ref):
    def save(v, level, value):
        surf_ref[v] = value

    stencil((0,), q_ref, m_ref, east_ref, west_ref, north_ref, south_ref, save)


def ocean_top(q, mask, edges):
    return pl.pallas_call(
        top_kernel,
        out_shape=jax.ShapeDtypeStruct((FIELDS,) + q.shape[1:], F32),
        in_specs=[spec_vmem()] * 6,
        out_specs=spec_vmem(),
        compiler_params=params(8),
        cost_estimate=pl.CostEstimate(flops=4 * q.size, bytes_accessed=q.size, transcendentals=0),
        name="ocean_top",
    )(q, mask, *edges)


def deep_kernel(q_ref, m_ref, east_ref, west_ref, north_ref, south_ref, top_ref, out_ref):
    depth = q_ref.shape[0] // FIELDS

    def save(v, level, value):
        out_ref[v * depth + level] = value

    for v in range(FIELDS):
        out_ref[v * depth] = top_ref[v]
    levels = range(1, depth)
    stencil(levels, q_ref, m_ref, east_ref, west_ref, north_ref, south_ref, save)


def ocean_deep(q, mask, edges, top):
    return pl.pallas_call(
        deep_kernel,
        out_shape=jax.ShapeDtypeStruct(q.shape, F32),
        in_specs=[spec_vmem()] * 7,
        out_specs=spec_vmem(),
        compiler_params=params(8),
        cost_estimate=pl.CostEstimate(
            flops=30 * q.size, bytes_accessed=8 * q.size, transcendentals=0
        ),
        name="ocean_deep",
    )(q, mask, *edges, top)


def combine_kernel(
    got_ref, bulk_ref, surf_ref, m_ref, resp_ref, top, back_ref
):
    rows = m_ref.shape[0]
    sources = back_ref.shape[0]
    chunk_rows = got_ref.shape[0] // sources
    table_rows = chunk_rows - FLUXES * CAP

    x = lax.broadcasted_iota(jnp.int32, (2 * rows, LANES), 0)
    spot = lax.broadcasted_iota(jnp.int32, (2 * rows, LANES), 1)
    pair = (spot // CAP) % 2 == x // rows
    wanted = jnp.where(pair, (x % rows + 1).astype(F32), -1.0)
    hots = []
    for j in range(table_rows):
        seen = got_ref[pl.ds(FLUXES * CAP + j, sources, stride=chunk_rows), :]
        seen = jnp.sum(seen, axis=0, keepdims=True)
        hots.append((seen == wanted).astype(F32))
    hot = jnp.concatenate([h.astype(BF16) for h in hots], axis=1)

    force = [None] * FIELDS
    for j in range(FLUXES // 2):
        data = jnp.concatenate(
            [got_ref[pl.ds(s * chunk_rows + j * SUB, SUB), :] for s in range(sources)], axis=0
        )
        high, low = halves(data)
        both = dot32(hot, high) + dot32(hot, low)
        for p in range(2):
            f = 2 * j + p
            drive = both[p * rows : (p + 1) * rows] * bulk_ref[f]
            for g in range(FIELDS):
                term = resp_ref[g * FLUXES + f, :][None, :] * drive
                force[g] = term if f == 0 else force[g] + term
    mask = m_ref[...].astype(F32)
    for g in range(FIELDS):
        top[g] = surf_ref[g] + mask * force[g]
    hot_t = jnp.concatenate([jnp.transpose(h).astype(BF16) for h in hots], axis=0)
    for j in range(FIELDS // 2):
        pair = jnp.concatenate([top[2 * j], top[2 * j + 1]], axis=0)
        high, low = halves(pair)
        both = dot32(hot_t, high) + dot32(hot_t, low)
        back_ref[:, j * SUB : (j + 1) * SUB, :] = both.reshape(sources, SUB, LANES)


def ocean_combine(got, bulk, surf, mask, response, sources):
    return pl.pallas_call(
        combine_kernel,
        out_shape=(
            jax.ShapeDtypeStruct(surf.shape, F32),
            jax.ShapeDtypeStruct((sources, FIELDS * CAP, LANES), F32),
        ),
        in_specs=[spec_vmem()] * 5,
        out_specs=(spec_vmem(), spec_vmem()),
        compiler_params=params(16),
        cost_estimate=pl.CostEstimate(
            flops=4 * got.size, bytes_accessed=4 * got.size, transcendentals=0
        ),
        name="ocean_combine",
    )(got, bulk, surf, mask, response)


def turn_kernel(w_ref, out_ref):
    for e in range(w_ref.shape[0]):
        out_ref[e] = jnp.transpose(w_ref[e])


def turn_blocks(weights):
    entries = weights.shape[0]
    per = 32
    spec = pl.BlockSpec((per,) + weights.shape[1:], lambda i: (i, 0, 0))
    return pl.pallas_call(
        turn_kernel,
        grid=(entries // per,),
        out_shape=jax.ShapeDtypeStruct(weights.shape, BF16),
        in_specs=[spec],
        out_specs=spec,
        compiler_params=params(58),
        cost_estimate=pl.CostEstimate(
            flops=weights.size, bytes_accessed=4 * weights.size, transcendentals=0
        ),
        name="turn_blocks",
    )(weights)


def regrid_kernel(got_ref, pick_ref, w_ref, tile_hbm, out_ref, parts, tile_ref, sem):
    entries = w_ref.shape[0]
    rows = got_ref.shape[0] * SUB
    copy = pltpu.make_async_copy(tile_hbm, tile_ref, sem)
    copy.start()
    out_ref[...] = jnp.zeros_like(out_ref)
    pick = pick_ref[...]
    for j in range(FIELDS // 2):
        data = got_ref[:, j * SUB : (j + 1) * SUB, :].reshape(rows, LANES)
        for h, half in enumerate(halves(data)):
            at = (h * FIELDS + 2 * j) * entries
            parts[at : at + 2 * entries, :] = dot32(pick, half)
    copy.wait()

    def group(i, _):
        results = []
        for u in range(SUB):
            e = i * SUB + u
            rows = parts[pl.ds(e, 2 * FIELDS, stride=entries), :]
            both = dot32(rows.astype(BF16), w_ref[e])
            results.append((tile_ref[e], both[:FIELDS] + both[FIELDS:]))
        for tile, value in results:
            out_ref[tile] = out_ref[tile] + value
        return 0

    lax.fori_loop(0, entries // SUB, group, 0, unroll=min(entries // SUB, 8))


def regrid_back(got, picks, turned, tile_ids, tiles):
    entries = turned.shape[0]
    return pl.pallas_call(
        regrid_kernel,
        out_shape=jax.ShapeDtypeStruct((tiles, FIELDS, LANES), F32),
        in_specs=[spec_vmem(), spec_vmem(), spec_vmem(), spec_any()],
        out_specs=spec_vmem(),
        scratch_shapes=[
            pltpu.VMEM((2 * FIELDS * entries, LANES), F32),
            pltpu.SMEM(tile_ids.shape, jnp.int32),
            pltpu.SemaphoreType.DMA,
        ],
        compiler_params=params(16),
        name="regrid_back",
    )(got, picks, turned, tile_ids)


def exchange(x):
    return lax.all_to_all(x, BOTH, split_axis=0, concat_axis=0, tiled=True)


def per_device(
    atm_state,
    diffusivity,
    surface_prev,
    flux_mix,
    entry_dest,
    entry_tile,
    entry_row,
    regrid_blocks,
    ocean_state,
    land_mask,
    flux_response,
):
    devices = lax.axis_size("sec") * lax.axis_size("tile")
    _, levels, columns = atm_state.shape
    blocks, tiles = levels // SUB, columns // LANES
    _, depth, rows, _ = ocean_state.shape

    a_tiles = atm_state.reshape(FIELDS, blocks, SUB, tiles, LANES).transpose(0, 1, 3, 2, 4)
    d_tiles = diffusivity.reshape(blocks, SUB, tiles, LANES).transpose(0, 2, 1, 3)
    s_rows = surface_prev.reshape(FIELDS, tiles, LANES).transpose(1, 0, 2)
    s_rows = s_rows.reshape(tiles * FIELDS, LANES)
    dest = entry_dest[:, 0]
    outgoing = atm_forward(
        a_tiles, d_tiles, s_rows, flux_mix, dest, entry_tile, entry_row, regrid_blocks, devices
    )

    q = ocean_state.reshape(FIELDS * depth, rows, LANES)
    outgoing, q, blocks_in = lax.optimization_barrier((outgoing, q, regrid_blocks))
    turned = turn_blocks(blocks_in)
    chunk_rows = outgoing.shape[0] // devices
    incoming = exchange(outgoing.reshape(devices, chunk_rows // 2, 2, LANES))
    incoming = incoming.reshape(outgoing.shape)

    low_row, high_row, low_col, high_col = ocean_edges(q, land_mask)
    edges = (
        lax.ppermute(low_row, "sec", shift("sec", -1)),
        lax.ppermute(high_row, "sec", shift("sec", 1)),
        lax.ppermute(low_col, "tile", shift("tile", -1)),
        lax.ppermute(high_col, "tile", shift("tile", 1)),
    )
    bulk, resp_rows, picks = ocean_bulk(q, flux_response, dest, devices)
    turned, edges = lax.optimization_barrier((turned, edges))
    surf = ocean_top(q, land_mask, edges)
    top, returning = ocean_combine(incoming, bulk, surf, land_mask, resp_rows, devices)
    arrived = exchange(returning)
    q_next = ocean_deep(q, land_mask, edges, top)
    q_next, a_tiles, d_tiles, s_rows = lax.optimization_barrier(
        (q_next, a_tiles, d_tiles, s_rows)
    )
    atm_next = atm_solve(a_tiles, d_tiles, s_rows).transpose(0, 1, 3, 2, 4).reshape(FIELDS, levels, columns)
    back = regrid_back(arrived, picks, turned, entry_tile, tiles)
    surface_next = back.transpose(1, 0, 2).reshape(FIELDS, columns)
    return atm_next, q_next.reshape(ocean_state.shape), surface_next


def solution(mesh):
    return jax.shard_map(
        per_device,
        mesh=mesh,
        in_specs=(
            P(None, None, BOTH),
            P(None, BOTH),
            P(None, BOTH),
            P(),
            P(BOTH, None),
            P(BOTH),
            P(BOTH),
            P(BOTH, None, None),
            P(None, None, "sec", "tile"),
            P("sec", "tile"),
            P(),
        ),
        out_specs=(
            P(None, None, BOTH),
            P(None, None, "sec", "tile"),
            P(None, BOTH),
        ),
        check_vma=False,
    )
```

```python
import functools

import jax
import jax.numpy as jnp
from jax import lax
from jax.experimental import pallas as pl
from jax.experimental.pallas import tpu as pltpu
from jax.sharding import PartitionSpec as P

CAP = 4
LANES = 128
SUB = 8
FLUXES = 10
FEATURES = 12
FIELDS = 4
DIFFUSE = 0.2
CORIOLIS = 0.3
OCEAN_DT = 0.2
F32 = jnp.float32
BF16 = jnp.bfloat16
BOTH = ("sec", "tile")


def halves(x):
    high = x.astype(BF16)
    return high, (x - high.astype(F32)).astype(BF16)


def dot32(a, b):
    return jnp.dot(a, b, preferred_element_type=F32)


def spec_any():
    return pl.BlockSpec(memory_space=pltpu.HBM)


def spec_vmem():
    return pl.BlockSpec(memory_space=pltpu.VMEM)


def spec_smem():
    return pl.BlockSpec(memory_space=pltpu.SMEM)


def params(mib):
    return pltpu.CompilerParams(vmem_limit_bytes=mib * 2**20)


def eliminate(a_rows, d_rows, surface, tiles, blocks, first, groups, keep):
    def block(step, carry):
        lb = blocks - 1 - step
        bottom = jnp.where(lb == 0, 1.0, 0.0).astype(F32)
        carry = list(carry)
        for r in range(SUB - 1, -1, -1):
            for g in range(groups):
                tile = first + g * SUB
                grow, above, ys = carry[g]
                coup = d_rows[pl.ds((lb * tiles + tile) * SUB + r, SUB, stride=SUB), :]
                weight = 1.0 + above * grow
                inverse = 1.0 / (weight + coup)
                solved = []
                for v in range(FIELDS):
                    row = ((v * blocks + lb) * tiles + tile) * SUB + r
                    rhs = a_rows[pl.ds(row, SUB, stride=SUB), :]
                    if r == 0:
                        rhs = rhs + coup * (surface(v, tile) * bottom)
                    solved.append((rhs + above * ys[v]) * inverse)
                keep(lb, r, tile, coup * inverse, solved)
                carry[g] = (weight * inverse, coup, tuple(solved))
        return tuple(carry)

    zero = jnp.zeros((SUB, LANES), F32)
    start = tuple((zero, zero, (zero,) * FIELDS) for _ in range(groups))
    final = lax.fori_loop(0, blocks, block, start)
    return [(coup, x0) for _, coup, x0 in final]


def atm_kernel(
    chunks,
    chunk_rows,
    a_ref,
    d_ref,
    s_ref,
    mix_hbm,
    dest_hbm,
    tile_hbm,
    row_hbm,
    w_ref,
    out_hbm,
    a_buf,
    d_buf,
    s_buf,
    w_buf,
    y_buf,
    e_buf,
    flux,
    out_ref,
    mix_ref,
    dest_ref,
    tile_ref,
    row_ref,
    count,
    in_sems,
    sems,
):
    blocks, tiles = a_buf.shape[1], a_buf.shape[2]
    entries = w_buf.shape[0]
    per = tiles // chunks
    groups = per // SUB
    devices = count.shape[0]
    table_rows = chunk_rows - FLUXES * CAP
    me = lax.axis_index("sec") * lax.axis_size("tile") + lax.axis_index("tile")

    def surface(v, tile):
        return s_buf[pl.ds(tile * FIELDS + v, SUB, stride=FIELDS), :]

    def loads(ci):
        at = pl.ds(ci * per, per)
        return (
            pltpu.make_async_copy(d_ref.at[:, at], d_buf.at[:, at], in_sems.at[ci, 0]),
            pltpu.make_async_copy(a_ref.at[:, :, at], a_buf.at[:, :, at], in_sems.at[ci, 1]),
        )

    small = [
        pltpu.make_async_copy(src, dst, sems.at[i])
        for i, (src, dst) in enumerate(
            (
                (s_ref, s_buf),
                (mix_hbm, mix_ref),
                (dest_hbm, dest_ref),
                (tile_hbm, tile_ref),
                (row_hbm, row_ref),
            )
        )
    ]
    w_copy = pltpu.make_async_copy(w_ref, w_buf, sems.at[5])
    for copy in loads(0):
        copy.start()
    for copy in small:
        copy.start()
    for ci in range(1, chunks):
        for copy in loads(ci):
            copy.start()
    w_copy.start()

    a_rows = a_buf.reshape(FIELDS * blocks * tiles * SUB, LANES)
    d_rows = d_buf.reshape(blocks * tiles * SUB, LANES)
    for d in range(devices):
        count[d] = 0
    out_ref[...] = jnp.zeros_like(out_ref)
    for copy in small:
        copy.wait()

    def keep(lb, r, tile, coef, solved):
        if r == 1:
            e_buf[pl.ds(tile, SUB), :] = coef
            for v in range(FIELDS):
                y_buf[v, pl.ds(tile, SUB), :] = solved[v]

    def chunk(ci, _):
        for copy in loads(ci):
            copy.wait()
        first = ci * per
        final = eliminate(a_rows, d_rows, surface, tiles, blocks, first, groups, keep)
        for g in range(groups):
            tile = first + g * SUB
            coup, x0 = final[g]
            e1 = e_buf[pl.ds(tile, SUB), :]
            turb = [coup * (surface(v, tile) - x0[v]) for v in range(FIELDS)]
            x1 = [y_buf[v, pl.ds(tile, SUB), :] + e1 * x0[v] for v in range(FIELDS)]
            feats = turb + list(x0) + [turb[v] * x1[v] for v in range(FIELDS)]
            for f in range(FLUXES):
                total = mix_ref[f, 0] * feats[0]
                for k in range(1, FEATURES):
                    total = total + mix_ref[f, k] * feats[k]
                flux[pl.ds(tile * 16 + f, SUB, stride=16), :] = total
        return 0

    lax.fori_loop(0, chunks, chunk, 0)
    w_copy.wait()

    spot = lax.broadcasted_iota(jnp.int32, (table_rows, LANES), 0) * LANES
    spot = spot + lax.broadcasted_iota(jnp.int32, (table_rows, LANES), 1)

    def entry(e, _):
        d = dest_ref[e]
        k = count[d]
        count[d] = k + 1
        hit = spot == me * CAP + k
        table = pl.ds(d * chunk_rows + FLUXES * CAP, table_rows)
        out_ref[table, :] += jnp.where(hit, row_ref[e] + 1, 0).astype(F32)
        picked = flux[pl.ds(pl.multiple_of(tile_ref[e] * 16, 16), 16), :]
        high, low = halves(picked)
        both = dot32(jnp.concatenate([high, low], axis=0), w_buf[e])
        both = both[:16] + both[16:]
        row = d * chunk_rows + k
        out_ref[pl.ds(row, SUB, stride=CAP), :] = both[:SUB]
        out_ref[pl.ds(row + SUB * CAP, FLUXES - SUB, stride=CAP), :] = both[SUB:FLUXES]
        return 0

    lax.fori_loop(0, entries, entry, 0, unroll=min(entries, 64))
    out_copy = pltpu.make_async_copy(out_ref, out_hbm, sems.at[6])
    out_copy.start()
    out_copy.wait()


def atm_forward(a_tiles, d_tiles, s_rows, mix, dest, tile_ids, row_ids, weights, devices):
    _, _, tiles, _, _ = a_tiles.shape
    entries = weights.shape[0]
    chunks = 4
    chunk_rows = FLUXES * CAP + devices * CAP // LANES
    out_shape = (devices * chunk_rows, LANES)
    return pl.pallas_call(
        functools.partial(atm_kernel, chunks, chunk_rows),
        out_shape=jax.ShapeDtypeStruct(out_shape, F32),
        in_specs=[spec_any()] * 8,
        out_specs=spec_any(),
        scratch_shapes=[
            pltpu.VMEM(a_tiles.shape, F32),
            pltpu.VMEM(d_tiles.shape, F32),
            pltpu.VMEM(s_rows.shape, F32),
            pltpu.VMEM(weights.shape, BF16),
            pltpu.VMEM((FIELDS, tiles, LANES), F32),
            pltpu.VMEM((tiles, LANES), F32),
            pltpu.VMEM((tiles * 16, LANES), F32),
            pltpu.VMEM(out_shape, F32),
            pltpu.SMEM(mix.shape, F32),
            pltpu.SMEM((entries,), jnp.int32),
            pltpu.SMEM((entries,), jnp.int32),
            pltpu.SMEM((entries,), jnp.int32),
            pltpu.SMEM((devices,), jnp.int32),
            pltpu.SemaphoreType.DMA((chunks, 2)),
            pltpu.SemaphoreType.DMA((7,)),
        ],
        compiler_params=params(60),
        name="atm_forward",
    )(a_tiles, d_tiles, s_rows, mix, dest, tile_ids, row_ids, weights)


def solve_kernel(a_ref, d_ref, s_ref, out_ref, y_buf, e_buf):
    blocks, tiles = out_ref.shape[1], out_ref.shape[2]
    a_rows = a_ref.reshape(FIELDS * blocks * tiles * SUB, LANES)
    d_rows = d_ref.reshape(blocks * tiles * SUB, LANES)
    rows = out_ref.reshape(FIELDS * blocks * tiles * SUB, LANES)
    groups = tiles // SUB

    def surface(v, tile):
        return s_ref[pl.ds(tile * FIELDS + v, SUB, stride=FIELDS), :]

    def keep(lb, r, tile, coef, solved):
        level = lb * SUB + r
        e_buf[level, pl.ds(tile, SUB), :] = coef
        for v in range(FIELDS):
            y_buf[v, level, pl.ds(tile, SUB), :] = solved[v]

    eliminate(a_rows, d_rows, surface, tiles, blocks, 0, groups, keep)

    def block(lb, carry):
        carry = list(carry)
        for r in range(SUB):
            for g in range(groups):
                coef = e_buf[lb * SUB + r, pl.ds(g * SUB, SUB), :]
                if r == 0:
                    coef = coef * jnp.where(lb == 0, 0.0, 1.0).astype(F32)
                for v in range(FIELDS):
                    x = y_buf[v, lb * SUB + r, pl.ds(g * SUB, SUB), :]
                    x = x + coef * carry[g * FIELDS + v]
                    row = ((v * blocks + lb) * tiles + g * SUB) * SUB + r
                    rows[pl.ds(row, SUB, stride=SUB), :] = x
                    carry[g * FIELDS + v] = x
        return tuple(carry)

    zero = jnp.zeros((SUB, LANES), F32)
    lax.fori_loop(0, blocks, block, (zero,) * (groups * FIELDS))


def atm_solve(a_tiles, d_tiles, s_rows):
    _, blocks, tiles, _, _ = a_tiles.shape
    levels = blocks * SUB
    per = 16
    return pl.pallas_call(
        solve_kernel,
        grid=(tiles // per,),
        out_shape=jax.ShapeDtypeStruct(a_tiles.shape, F32),
        in_specs=[
            pl.BlockSpec((FIELDS, blocks, per, SUB, LANES), lambda i: (0, 0, i, 0, 0)),
            pl.BlockSpec((blocks, per, SUB, LANES), lambda i: (0, i, 0, 0)),
            pl.BlockSpec((per * FIELDS, LANES), lambda i: (i, 0)),
        ],
        out_specs=pl.BlockSpec((FIELDS, blocks, per, SUB, LANES), lambda i: (0, 0, i, 0, 0)),
        scratch_shapes=[
            pltpu.VMEM((FIELDS, levels, per, LANES), F32),
            pltpu.VMEM((levels, per, LANES), F32),
        ],
        compiler_params=params(60),
        cost_estimate=pl.CostEstimate(
            flops=8 * a_tiles.size, bytes_accessed=9 * a_tiles.size, transcendentals=0
        ),
        name="atm_solve",
    )(a_tiles, d_tiles, s_rows)


def edge_kernel(q_ref, m_ref, low_row, high_row, low_col, high_col):
    fields, rows, _ = q_ref.shape
    mask = m_ref[...].astype(F32)
    for dst, at in ((low_row, 0), (high_row, rows - 1)):
        dst[...] = jnp.zeros_like(dst)
        for i in range(fields):
            dst[i : i + 1, :] = q_ref[i, at : at + 1, :]
        dst[fields : fields + 1, :] = mask[at : at + 1, :]

    lane = lax.broadcasted_iota(jnp.int32, (rows, LANES), 1)
    low = jnp.zeros((rows, LANES), F32)
    high = jnp.zeros((rows, LANES), F32)
    for i in range(fields + 1):
        cells = q_ref[i] if i < fields else mask
        turned = pltpu.roll(cells, i, 1) if i else cells
        low = jnp.where(lane == i, turned, low)
        high = jnp.where(lane == (i + LANES - 1) % LANES, turned, high)
    low_col[...] = low
    high_col[...] = high


def ocean_edges(q, mask):
    pad = -(-(q.shape[0] + 1) // SUB) * SUB
    row = jax.ShapeDtypeStruct((pad, LANES), F32)
    col = jax.ShapeDtypeStruct(mask.shape, F32)
    return pl.pallas_call(
        edge_kernel,
        out_shape=(row, row, col, col),
        in_specs=[spec_vmem(), spec_vmem()],
        out_specs=(spec_vmem(),) * 4,
        compiler_params=params(8),
        cost_estimate=pl.CostEstimate(flops=q.size, bytes_accessed=4 * q.size, transcendentals=0),
        name="ocean_edges",
    )(q, mask)


def shift(axis, step):
    count = lax.axis_size(axis)
    if step > 0:
        return [(i, i + 1) for i in range(count - 1)]
    return [(i + 1, i) for i in range(count - 1)]


def bulk_kernel(q_ref, resp_ref, dest_ref, bulk_ref, rows_ref, pick_ref, wide, count):
    depth = q_ref.shape[0] // FIELDS
    for g in range(FIELDS):
        for f in range(FLUXES):
            i = g * FLUXES + f
            rows_ref[i : i + 1, :] = jnp.full((1, LANES), resp_ref[g, f], F32)
    tops = [q_ref[v * depth] for v in range(FIELDS)]
    for f in range(FLUXES):
        total = resp_ref[0, f] * tops[0]
        for v in range(1, FIELDS):
            total = total + resp_ref[v, f] * tops[v]
        bulk_ref[f] = 1.0 + 0.5 * jnp.tanh(total)

    entries = dest_ref.shape[0]
    lane = lax.broadcasted_iota(jnp.int32, (1, wide.shape[1]), 1)
    for d in range(count.shape[0]):
        count[d] = 0

    def entry(e, _):
        d = dest_ref[e]
        k = count[d]
        count[d] = k + 1
        for p in range(2):
            here = d * (2 * CAP) + p * CAP + k
            wide[pl.ds(p * entries + e, 1), :] = (lane == here).astype(F32)
        return 0

    lax.fori_loop(0, entries, entry, 0, unroll=4)
    pick_ref[...] = wide[...].astype(BF16)


def ocean_bulk(q, response, dest, devices):
    picks = (2 * dest.shape[0], devices * 2 * CAP)
    return pl.pallas_call(
        bulk_kernel,
        out_shape=(
            jax.ShapeDtypeStruct((FLUXES,) + q.shape[1:], F32),
            jax.ShapeDtypeStruct((FIELDS * FLUXES, LANES), F32),
            jax.ShapeDtypeStruct(picks, BF16),
        ),
        in_specs=[spec_vmem(), spec_smem(), spec_smem()],
        out_specs=(spec_vmem(),) * 3,
        scratch_shapes=[pltpu.VMEM(picks, F32), pltpu.SMEM((devices,), jnp.int32)],
        compiler_params=params(8),
        cost_estimate=pl.CostEstimate(
            flops=3 * q.size, bytes_accessed=2 * q.size, transcendentals=q.size // 3
        ),
        name="ocean_bulk",
    )(q, response, dest)


def stencil(levels, q_ref, m_ref, east_ref, west_ref, north_ref, south_ref, save):
    fields, rows, _ = q_ref.shape
    depth = fields // FIELDS
    lane = lax.broadcasted_iota(jnp.int32, (rows, LANES), 1)
    last, first = lane == LANES - 1, lane == 0

    def around(cells, i):
        high = (i + LANES - 1) % LANES
        east = jnp.concatenate([cells[1:], east_ref[i : i + 1, :]], axis=0)
        west = jnp.concatenate([west_ref[i : i + 1, :], cells[:-1]], axis=0)
        north = jnp.where(last, north_ref[:, i : i + 1], pltpu.roll(cells, LANES - 1, 1))
        south = jnp.where(first, south_ref[:, high : high + 1], pltpu.roll(cells, 1, 1))
        return east, west, north, south

    mask = m_ref[...].astype(F32)
    m_east, m_west, m_north, m_south = around(mask, fields)
    m_all = m_east + m_west + m_north + m_south
    for level in levels:
        zonal = q_ref[2 * depth + level]
        merid = q_ref[3 * depth + level]
        for v in range(FIELDS):
            i = v * depth + level
            cells = q_ref[i]
            east, west, north, south = around(cells, i)
            lap = m_east * east + m_west * west + m_north * north + m_south * south
            lap = lap - m_all * cells
            adv = 0.5 * (zonal * (east - west) + merid * (north - south))
            tend = DIFFUSE * lap - adv
            if v == 2:
                tend = tend + CORIOLIS * merid
            if v == 3:
                tend = tend - CORIOLIS * zonal
            save(v, level, mask * (cells + OCEAN_DT * tend))


def top_kernel(q_ref, m_ref, east_ref, west_ref, north_ref, south_ref, surf_ref):
    def save(v, level, value):
        surf_ref[v] = value

    stencil((0,), q_ref, m_ref, east_ref, west_ref, north_ref, south_ref, save)


def ocean_top(q, mask, edges):
    return pl.pallas_call(
        top_kernel,
        out_shape=jax.ShapeDtypeStruct((FIELDS,) + q.shape[1:], F32),
        in_specs=[spec_vmem()] * 6,
        out_specs=spec_vmem(),
        compiler_params=params(8),
        cost_estimate=pl.CostEstimate(flops=4 * q.size, bytes_accessed=q.size, transcendentals=0),
        name="ocean_top",
    )(q, mask, *edges)


def deep_kernel(q_ref, m_ref, east_ref, west_ref, north_ref, south_ref, top_ref, out_ref):
    depth = q_ref.shape[0] // FIELDS

    def save(v, level, value):
        out_ref[v * depth + level] = value

    for v in range(FIELDS):
        out_ref[v * depth] = top_ref[v]
    levels = range(1, depth)
    stencil(levels, q_ref, m_ref, east_ref, west_ref, north_ref, south_ref, save)


def ocean_deep(q, mask, edges, top):
    return pl.pallas_call(
        deep_kernel,
        out_shape=jax.ShapeDtypeStruct(q.shape, F32),
        in_specs=[spec_vmem()] * 7,
        out_specs=spec_vmem(),
        compiler_params=params(8),
        cost_estimate=pl.CostEstimate(
            flops=30 * q.size, bytes_accessed=8 * q.size, transcendentals=0
        ),
        name="ocean_deep",
    )(q, mask, *edges, top)


def combine_kernel(
    got_ref, bulk_ref, surf_ref, m_ref, resp_ref, top, back_ref
):
    rows = m_ref.shape[0]
    sources = back_ref.shape[0]
    chunk_rows = got_ref.shape[0] // sources
    table_rows = chunk_rows - FLUXES * CAP

    x = lax.broadcasted_iota(jnp.int32, (2 * rows, LANES), 0)
    spot = lax.broadcasted_iota(jnp.int32, (2 * rows, LANES), 1)
    pair = (spot // CAP) % 2 == x // rows
    wanted = jnp.where(pair, (x % rows + 1).astype(F32), -1.0)
    lane_in = lax.broadcasted_iota(jnp.int32, (LANES, LANES), 0)
    lane_out = lax.broadcasted_iota(jnp.int32, (LANES, LANES), 1)
    twice = lane_out // (2 * CAP) * CAP + lane_out % CAP
    hots = []
    for j in range(table_rows):
        seen = got_ref[pl.ds(FLUXES * CAP + j, sources, stride=chunk_rows), :]
        seen = jnp.sum(seen, axis=0, keepdims=True)
        seen = jnp.broadcast_to(seen, (SUB, LANES)).astype(BF16)
        for p in range(2):
            spread = (lane_in == twice + p * (LANES // 2)).astype(F32).astype(BF16)
            hots.append((dot32(seen, spread)[0:1] == wanted).astype(F32))
    hot = jnp.concatenate([h.astype(BF16) for h in hots], axis=1)

    force = [None] * FIELDS
    for j in range(FLUXES // 2):
        data = jnp.concatenate(
            [got_ref[pl.ds(s * chunk_rows + j * SUB, SUB), :] for s in range(sources)], axis=0
        )
        high, low = halves(data)
        both = dot32(hot, high) + dot32(hot, low)
        for p in range(2):
            f = 2 * j + p
            drive = both[p * rows : (p + 1) * rows] * bulk_ref[f]
            for g in range(FIELDS):
                term = resp_ref[g * FLUXES + f, :][None, :] * drive
                force[g] = term if f == 0 else force[g] + term
    mask = m_ref[...].astype(F32)
    for g in range(FIELDS):
        top[g] = surf_ref[g] + mask * force[g]
    hot_t = jnp.concatenate([jnp.transpose(h).astype(BF16) for h in hots], axis=0)
    for j in range(FIELDS // 2):
        pair = jnp.concatenate([top[2 * j], top[2 * j + 1]], axis=0)
        high, low = halves(pair)
        both = dot32(hot_t, high) + dot32(hot_t, low)
        back_ref[:, j * SUB : (j + 1) * SUB, :] = both.reshape(sources, SUB, LANES)


def ocean_combine(got, bulk, surf, mask, response, sources):
    return pl.pallas_call(
        combine_kernel,
        out_shape=(
            jax.ShapeDtypeStruct(surf.shape, F32),
            jax.ShapeDtypeStruct((sources, FIELDS * CAP, LANES), F32),
        ),
        in_specs=[spec_vmem()] * 5,
        out_specs=(spec_vmem(), spec_vmem()),
        compiler_params=params(16),
        cost_estimate=pl.CostEstimate(
            flops=4 * got.size, bytes_accessed=4 * got.size, transcendentals=0
        ),
        name="ocean_combine",
    )(got, bulk, surf, mask, response)


def turn_kernel(w_ref, out_ref):
    for e in range(w_ref.shape[0]):
        out_ref[e] = jnp.transpose(w_ref[e])


def turn_blocks(weights):
    entries = weights.shape[0]
    per = 32
    spec = pl.BlockSpec((per,) + weights.shape[1:], lambda i: (i, 0, 0))
    return pl.pallas_call(
        turn_kernel,
        grid=(entries // per,),
        out_shape=jax.ShapeDtypeStruct(weights.shape, BF16),
        in_specs=[spec],
        out_specs=spec,
        compiler_params=params(58),
        cost_estimate=pl.CostEstimate(
            flops=weights.size, bytes_accessed=4 * weights.size, transcendentals=0
        ),
        name="turn_blocks",
    )(weights)


def regrid_kernel(got_ref, pick_ref, w_ref, tile_hbm, out_ref, parts, tile_ref, sem):
    entries = w_ref.shape[0]
    rows = got_ref.shape[0] * SUB
    copy = pltpu.make_async_copy(tile_hbm, tile_ref, sem)
    copy.start()
    out_ref[...] = jnp.zeros_like(out_ref)
    pick = pick_ref[...]
    for j in range(FIELDS // 2):
        data = got_ref[:, j * SUB : (j + 1) * SUB, :].reshape(rows, LANES)
        for h, half in enumerate(halves(data)):
            at = (h * FIELDS + 2 * j) * entries
            parts[at : at + 2 * entries, :] = dot32(pick, half)
    copy.wait()

    def group(i, _):
        results = []
        for u in range(SUB):
            e = i * SUB + u
            rows = parts[pl.ds(e, 2 * FIELDS, stride=entries), :]
            both = dot32(rows.astype(BF16), w_ref[e])
            results.append((tile_ref[e], both[:FIELDS] + both[FIELDS:]))
        for tile, value in results:
            out_ref[tile] = out_ref[tile] + value
        return 0

    lax.fori_loop(0, entries // SUB, group, 0, unroll=min(entries // SUB, 8))


def regrid_back(got, picks, turned, tile_ids, tiles):
    entries = turned.shape[0]
    return pl.pallas_call(
        regrid_kernel,
        out_shape=jax.ShapeDtypeStruct((tiles, FIELDS, LANES), F32),
        in_specs=[spec_vmem(), spec_vmem(), spec_vmem(), spec_any()],
        out_specs=spec_vmem(),
        scratch_shapes=[
            pltpu.VMEM((2 * FIELDS * entries, LANES), F32),
            pltpu.SMEM(tile_ids.shape, jnp.int32),
            pltpu.SemaphoreType.DMA,
        ],
        compiler_params=params(16),
        name="regrid_back",
    )(got, picks, turned, tile_ids)


def exchange(x):
    return lax.all_to_all(x, BOTH, split_axis=0, concat_axis=0, tiled=True)


def per_device(
    atm_state,
    diffusivity,
    surface_prev,
    flux_mix,
    entry_dest,
    entry_tile,
    entry_row,
    regrid_blocks,
    ocean_state,
    land_mask,
    flux_response,
):
    devices = lax.axis_size("sec") * lax.axis_size("tile")
    _, levels, columns = atm_state.shape
    blocks, tiles = levels // SUB, columns // LANES
    _, depth, rows, _ = ocean_state.shape

    a_tiles = atm_state.reshape(FIELDS, blocks, SUB, tiles, LANES).transpose(0, 1, 3, 2, 4)
    d_tiles = diffusivity.reshape(blocks, SUB, tiles, LANES).transpose(0, 2, 1, 3)
    s_rows = surface_prev.reshape(FIELDS, tiles, LANES).transpose(1, 0, 2)
    s_rows = s_rows.reshape(tiles * FIELDS, LANES)
    dest = entry_dest[:, 0]
    outgoing = atm_forward(
        a_tiles, d_tiles, s_rows, flux_mix, dest, entry_tile, entry_row, regrid_blocks, devices
    )

    q = ocean_state.reshape(FIELDS * depth, rows, LANES)
    outgoing, q, blocks_in = lax.optimization_barrier((outgoing, q, regrid_blocks))
    turned = turn_blocks(blocks_in)
    chunk_rows = outgoing.shape[0] // devices
    incoming = exchange(outgoing.reshape(devices, chunk_rows, 1, LANES))
    incoming = incoming.reshape(outgoing.shape)

    low_row, high_row, low_col, high_col = ocean_edges(q, land_mask)
    edges = (
        lax.ppermute(low_row, "sec", shift("sec", -1)),
        lax.ppermute(high_row, "sec", shift("sec", 1)),
        lax.ppermute(low_col, "tile", shift("tile", -1)),
        lax.ppermute(high_col, "tile", shift("tile", 1)),
    )
    bulk, resp_rows, picks = ocean_bulk(q, flux_response, dest, devices)
    turned, edges = lax.optimization_barrier((turned, edges))
    surf = ocean_top(q, land_mask, edges)
    top, returning = ocean_combine(incoming, bulk, surf, land_mask, resp_rows, devices)
    arrived = exchange(returning)
    q_next = ocean_deep(q, land_mask, edges, top)
    q_next, a_tiles, d_tiles, s_rows = lax.optimization_barrier(
        (q_next, a_tiles, d_tiles, s_rows)
    )
    atm_next = atm_solve(a_tiles, d_tiles, s_rows).transpose(0, 1, 3, 2, 4).reshape(FIELDS, levels, columns)
    back = regrid_back(arrived, picks, turned, entry_tile, tiles)
    surface_next = back.transpose(1, 0, 2).reshape(FIELDS, columns)
    return atm_next, q_next.reshape(ocean_state.shape), surface_next


def solution(mesh):
    return jax.shard_map(
        per_device,
        mesh=mesh,
        in_specs=(
            P(None, None, BOTH),
            P(None, BOTH),
            P(None, BOTH),
            P(),
            P(BOTH, None),
            P(BOTH),
            P(BOTH),
            P(BOTH, None, None),
            P(None, None, "sec", "tile"),
            P("sec", "tile"),
            P(),
        ),
        out_specs=(
            P(None, None, BOTH),
            P(None, None, "sec", "tile"),
            P(None, BOTH),
        ),
        check_vma=False,
    )
```
